32 devices in a mesh: slab: 8 (over z, x), row: 4 (over y, core).
Axes of the slice: x: 2, y: 2, z: 4, core: 2. Of those that a mesh axis runs over, the one named last changes fastest.
Arguments:
- image: bfloat16 [32, 128, 8], P('slab', 'row'), may hold values from -6 to 6
- first_kernel: bfloat16 [3, 3, 32, 1], replicated, may hold values from -2 to 2
- first_bias: float32 [32], replicated, may hold values from -1.5 to 1.5
- middle_kernel: bfloat16 [3, 3, 32, 32], replicated, may hold values from -0.5 to 0.5
- middle_bias: float32 [32], replicated, may hold values from -1.5 to 1.5
- last_kernel: bfloat16 [3, 3, 3, 32], replicated, may hold values from -0.5 to 0.5
- last_bias: float32 [3], replicated, may hold values from -2 to 2
Outputs:
- flows: float32 [4, 32, 128, 8], P(None, 'slab', 'row')
The draws below stay inside these ranges and needn't reach their ends.
All inputs are finite; a program needn't handle non-finite values.
Results may differ from the reference program's by a relative error of at most 0.0052.
Values may be sent and summed in bfloat16 or wider, within the bound.
No kernel may reach another device: no remote copies, remote signals or barrier semaphores. Data moves between devices by JAX's collectives and lax.ppermute only.
A program may use at most 64 MiB of HBM per device.

```python
import jax
import jax.numpy as jnp
from jax import lax

CH = 32
Z = 32
Y = 128
X = 8


def levels(stream_key, dims, shards, least, largest):
    level = 1.0
    for position, parts in shards:
        heights = jax.random.uniform(jax.random.fold_in(jax.random.fold_in(stream_key, 6), position), (parts,), jnp.float32, least / len(shards), largest / len(shards))
        level = level * jnp.repeat(jnp.exp(heights), dims[position] // parts).reshape((-1,) + (1,) * (len(dims) - 1 - position))
    return level


def noise(stream_key, shape, spread, reach, pieces=(), kind=jnp.bfloat16):
    drawn = spread * jax.random.normal(stream_key, shape, jnp.float32)
    if pieces:
        drawn = drawn * levels(stream_key, shape, pieces, -0.22, 0.18)
    return jnp.clip(drawn, -reach, reach).astype(kind)


def setup_inputs(seed: int = 0) -> dict:
    key_of = jax.random.split(jax.random.key(seed), 8)
    return {
        "image": noise(key_of[0], (Z, Y, X), 1.0, 6.0, ((0, 8), (1, 4))),
        "first_kernel": noise(key_of[1], (3, 3, CH, 1), 9 ** -0.5, 2.0),
        "first_bias": noise(key_of[2], (CH,), 0.3, 1.5, (), jnp.float32),
        "middle_kernel": noise(key_of[3], (3, 3, CH, CH), (9 * CH // 2) ** -0.5, 0.5),
        "middle_bias": noise(key_of[4], (CH,), 0.3, 1.5, (), jnp.float32),
        "last_kernel": noise(key_of[5], (3, 3, 3, CH), (9 * CH // 2) ** -0.5, 0.5),
        "last_bias": noise(key_of[6], (3,), 0.5, 2.0, (), jnp.float32),
    }


def convolve(values, kernel):
    return lax.conv_general_dilated(values, kernel.astype(jnp.float32), (1, 1), ((1, 1), (1, 1)),
                                    dimension_numbers=("NCHW", "HWOI", "NCHW"),
                                    precision=lax.Precision.HIGHEST)


def network(planes, params):
    first_kernel, first_bias, middle_kernel, middle_bias, last_kernel, last_bias = params
    hidden_one = jax.nn.relu(convolve(planes[:, None].astype(jnp.float32), first_kernel)
                             + first_bias[None, :, None, None]).astype(jnp.bfloat16)
    hidden_two = jax.nn.relu(convolve(hidden_one.astype(jnp.float32), middle_kernel)
                             + middle_bias[None, :, None, None]).astype(jnp.bfloat16)
    return convolve(hidden_two.astype(jnp.float32), last_kernel) + last_bias[None, :, None, None]


def reference(image, first_kernel, first_bias, middle_kernel, middle_bias, last_kernel, last_bias):
    params = (first_kernel, first_bias, middle_kernel, middle_bias, last_kernel, last_bias)

    def single(plane):
        return network(plane[None], params)[0]

    xy_flows = lax.map(single, image, batch_size=8)
    yz_flows = lax.map(single, image.transpose(2, 0, 1), batch_size=8)
    yz_zero = yz_flows[:, 0].transpose(1, 2, 0)
    yz_one = yz_flows[:, 1].transpose(1, 2, 0)
    yz_two = yz_flows[:, 2].transpose(1, 2, 0)
    return jnp.stack([yz_zero, 0.5 * (xy_flows[:, 0] + yz_one), xy_flows[:, 1],
                      0.5 * (xy_flows[:, 2] + yz_two)])
```

```python
import functools

import jax
import jax.numpy as jnp
from jax import lax
from jax.experimental import pallas as pl
from jax.experimental.pallas import tpu as pltpu
from jax.sharding import PartitionSpec as P

SUB = 8
LANES = 128
NEVER = -3.0e38
LIMIT = 12 << 20
F32 = jnp.float32
BF16 = jnp.bfloat16


def matching(count, parity):
    partner = {}
    for left in range(parity, count - 1, 2):
        partner[left] = left + 1
        partner[left + 1] = left
    return partner


def swap_rows(values, parity):
    count = lax.axis_size("row")
    partner = matching(count, parity)
    ends = [i for i in range(count) if i not in partner]
    for here, there in zip(ends, reversed(ends)):
        partner[here] = there
    return lax.ppermute(values, "row", sorted(partner.items()))


def swap_slabs(values, parity):
    slabs, rows = lax.axis_size("slab"), lax.axis_size("row")
    partner = matching(slabs, parity)
    across = matching(rows, 0)
    pairs = []
    for s in range(slabs):
        for r in range(rows):
            there = (partner[s], r) if s in partner else (s, across.get(r, r))
            pairs.append((s * rows + r, there[0] * rows + there[1]))
    return lax.ppermute(values, ("slab", "row"), pairs)


def before_and_after(even, odd, axis):
    here, count = lax.axis_index(axis), lax.axis_size(axis)
    low = here % 2 == 0
    before = jnp.where(low, odd, even)
    after = jnp.where(low, even, odd)
    before = jnp.where(here > 0, before, jnp.zeros_like(before))
    after = jnp.where(here < count - 1, after, jnp.zeros_like(after))
    return before, after


def tile_lanes(row, count):
    return jnp.concatenate([row] * count, axis=1)


def iota(shape, dim):
    return lax.broadcasted_iota(jnp.int32, shape, dim)


def nn(left, right):
    return lax.dot_general(left, right, (((1,), (0,)), ((), ())), preferred_element_type=F32)


def nt(left, right):
    return lax.dot_general(left, right, (((1,), (1,)), ((), ())), preferred_element_type=F32)


def keep_hidden(scratch, values):
    for i in range(0, values.shape[1], LANES):
        piece = values[:, i : i + LANES]
        scratch[i // LANES][:, : piece.shape[1]] = piece


def gather_hidden(scratch, starts, count, lanes):
    columns = []
    for i in range(0, lanes, LANES):
        parts = [scratch[i // LANES][pl.ds(start, count, stride=SUB), :] for start in starts]
        columns.append(jnp.concatenate(parts, axis=0).astype(BF16)[:, : lanes - i])
    return jnp.concatenate(columns, axis=1)


class Sizes:
    def __init__(self, slices, rows, cols, channels, outputs, slabs, parts):
        self.slices, self.rows, self.cols = slices, rows, cols
        self.channels, self.outputs = channels, outputs
        self.slabs, self.parts = slabs, parts
        assert slices >= 3 and SUB % slices == 0
        self.halves = SUB // slices
        assert rows % self.halves == 0 and cols % SUB == 0
        self.span = rows // self.halves
        self.chunks = []
        self.kinds = []
        for start in range(0, cols, SUB):
            ranges = []
            for reach in (3, 2, 1, 0):
                low = max(0, start - reach)
                ranges.append((low - start, min(cols, start + SUB + reach) - low))
            kind = tuple(ranges)
            if kind not in self.kinds:
                self.kinds.append(kind)
            self.chunks.append((start, self.kinds.index(kind)))

    def weight_shapes(self):
        c, z = self.channels, self.slices
        shapes = [
            ((3, 3 * z * SUB, (z + 4) * c), BF16),
            ((3, (z + 2) * c, (z + 4) * c), BF16),
            ((3, self.outputs * z, (z + 2) * c), BF16),
            ((1, (z + 4) * c), F32),
            ((1, (z + 2) * c), F32),
        ]
        for image, one, two, _ in self.kinds:
            shapes += [
                ((3, z * image[1], one[1] * c), BF16),
                ((3, two[1] * c, one[1] * c), BF16),
                ((3, self.outputs * SUB, two[1] * c), BF16),
                ((1, one[1] * c), F32),
                ((1, two[1] * c), F32),
            ]
        return shapes + [((self.outputs, SUB, self.rows), F32)]


def banded(blocks, out_count, in_count, offset):
    zero = jnp.zeros_like(blocks[0])
    lines = []
    for out in range(out_count):
        line = []
        for inner in range(in_count):
            tap = inner - out + offset
            line.append(blocks[tap] if 0 <= tap < 3 else zero)
        lines.append(jnp.concatenate(line, axis=1))
    return jnp.concatenate(lines, axis=0)


def spread(rows_of, tap_of, shape, lines):
    total = jnp.zeros(shape, F32)
    for (group, tap), line in lines.items():
        here = tap_of == tap
        if rows_of is not None:
            here = here & (rows_of == group)
        total = jnp.where(here, line, total)
    return total.astype(BF16)


def prepare_kernel(sizes, t_ref, k1_ref, b1_ref, k2_ref, b2_ref, k3_ref, b3_ref, t_out, *outs):
    c, z, n_out = sizes.channels, sizes.slices, sizes.outputs
    t_out[...] = t_ref[...]
    k1 = k1_ref[...].astype(F32)
    k3 = k3_ref[...].astype(F32)
    b1, b2 = b1_ref[...], b2_ref[...]

    def first(shape, tap_of, tap_index):
        count = shape[1] // c
        lines = {(0, t): tile_lanes(k1[tap_index(t)[0], tap_index(t)[1]][None, :], count) for t in range(3)}
        return spread(None, tap_of, shape, lines)

    def last(shape, group_of, tap_of, tap_index):
        count = shape[1] // c
        lines = {}
        for g in range(n_out):
            for t in range(3):
                a, b = tap_index(t)
                lines[g, t] = tile_lanes(k3[a, b, g][None, :], count)
        return spread(group_of, tap_of, shape, lines)

    w1, w2, w3, c1, c2 = outs[:5]
    for b in range(3):
        shape = w1.shape[1:]
        tap = iota(shape, 0) // SUB - iota(shape, 1) // c + (3 - z)
        w1[b] = first(shape, tap, lambda t, b=b: (t, b))
        w2[b] = banded([k2_ref[a, b] for a in range(3)], z + 2, z + 4, 0)
        shape = w3.shape[1:]
        row = iota(shape, 0)
        w3[b] = last(shape, row // z, iota(shape, 1) // c - row % z, lambda t, b=b: (t, b))
    base = lax.axis_index("slab") * z
    for ref, bias, reach in ((c1, b1, 2), (c2, b2, 1)):
        where = base + iota(ref.shape, 1) // c - reach
        inside = (where >= 0) & (where < sizes.slabs * z)
        ref[...] = jnp.where(inside, tile_lanes(bias, ref.shape[1] // c), NEVER)

    for index, (image, one, two, out) in enumerate(sizes.kinds):
        w1, w2, w3, c1, c2 = outs[5 + 5 * index : 10 + 5 * index]
        for a in range(3):
            shape = w1.shape[1:]
            tap = iota(shape, 0) % image[1] + image[0] - iota(shape, 1) // c - one[0] + 1
            w1[a] = first(shape, tap, lambda t, a=a: (a, t))
            w2[a] = banded([k2_ref[a, b] for b in range(3)], two[1], one[1], one[0] - two[0] + 1)
            shape = w3.shape[1:]
            row = iota(shape, 0)
            tap = iota(shape, 1) // c + two[0] - row % SUB - out[0] + 1
            w3[a] = last(shape, row // SUB, tap, lambda t, a=a: (a, t))
        c1[...] = tile_lanes(b1, one[1])
        c2[...] = tile_lanes(b2, two[1])
    for g in range(n_out):
        outs[-1][g] = jnp.broadcast_to(b3_ref[0:1, g : g + 1], (SUB, sizes.rows))


def extend_kernel(own_ref, even_ref, odd_ref, out_ref):
    rows = own_ref.shape[2]
    before, after = before_and_after(even_ref[...], odd_ref[...], "row")
    out_ref[...] = jnp.concatenate([before[:, :, rows - 3 :], own_ref[...], after[:, :, :3]], axis=2)


def zero_groups(values, count, low, high):
    edge = count * SUB
    top, middle, bottom = values[:edge], values[edge:-edge], values[-edge:]
    if low.ndim:
        low, high = low[:edge], high[:edge]
    return jnp.concatenate([jnp.where(low, 0.0, top), middle, jnp.where(high, 0.0, bottom)], axis=0)


def taps(values, count):
    low, high = values.astype(BF16), values[SUB:].astype(BF16)
    return [low[:count], high[:count], low[2 * SUB : 2 * SUB + count]]


def hidden_layers(picked, groups, w1, w2, c1, c2, low, high):
    n1, n2 = (groups - 2) * SUB, (groups - 4) * SUB
    one = sum(nn(tap, w1[i]) for i, tap in enumerate(taps(picked, n1)))
    one = zero_groups(jnp.maximum(one + c1[...], 0.0), 2, low, high)
    two = sum(nt(tap, w2[i]) for i, tap in enumerate(taps(one, n2)))
    return zero_groups(jnp.maximum(two + c2[...], 0.0), 1, low, high)


def xy_kernel(sizes, e_ref, *refs):
    count = sum(1 for _ in sizes.kinds) * 5
    weights, (b3, out_ref, *hidden) = refs[:count], refs[count:]
    z, span = sizes.slices, sizes.span
    wide = sizes.rows + 6
    groups = span + 6
    row = lax.axis_index("row")
    half = iota((2 * SUB, 1), 0) % SUB // z
    low = (row == 0) & (half == 0)
    high = (row == sizes.parts - 1) & (half == sizes.halves - 1)
    shape = (groups * SUB, wide)
    wanted = iota(shape, 0) // SUB + iota(shape, 0) % SUB // z * span
    select = jnp.where(iota(shape, 1) == wanted, 1.0, 0.0).astype(BF16)
    for start, index in sizes.chunks:
        image = sizes.kinds[index][0]
        w1, w2, w3, c1, c2 = weights[5 * index : 5 * index + 5]
        low_col = start + image[0]
        e = e_ref[:, low_col : low_col + image[1], :].reshape(z * image[1], wide)
        picked = nt(select, e)
        same = iota(picked.shape, 1) // image[1] == iota(picked.shape, 0) % z
        picked = jnp.where(same, picked, 0.0)
        second = hidden_layers(picked, groups, w1, w2, c1, c2, low, high)
        keep_hidden(hidden, second)
        total = None
        for a in range(3):
            starts = [SUB * a + h * z + s for s in range(z) for h in range(sizes.halves)]
            term = nt(w3[a], gather_hidden(hidden, starts, span, second.shape[1]))
            total = term if total is None else total + term
        for g in range(sizes.outputs):
            for s in range(z):
                piece = total[g * SUB : (g + 1) * SUB, s * sizes.rows : (s + 1) * sizes.rows]
                out_ref[g, s, start : start + SUB, :] = piece + b3[g]


def yz_kernel(sizes, e_ref, even_ref, odd_ref, xy_ref, w1, w2, w3, c1, c2, b3, out_ref, turned, *hidden):
    z = sizes.slices
    wide = sizes.rows + 6
    groups = sizes.rows + 6
    row = lax.axis_index("row")
    low, high = row == 0, row == sizes.parts - 1
    before, after = before_and_after(even_ref[...], odd_ref[...], "slab")
    block = jnp.concatenate([before, e_ref[...], after], axis=0)
    shape = (groups * SUB, wide)
    select = jnp.where(iota(shape, 1) == iota(shape, 0) // SUB, 1.0, 0.0).astype(BF16)
    for start in range(0, sizes.cols, SUB):
        e = block[:, start : start + SUB, :].reshape(3 * z * SUB, wide)
        picked = nt(select, e)
        same = iota(picked.shape, 1) % SUB == iota(picked.shape, 0) % SUB
        picked = jnp.where(same, picked, 0.0)
        two = hidden_layers(picked, groups, w1, w2, c1, c2, low, high)
        keep_hidden(hidden, two)
        total = None
        for b in range(3):
            starts = [SUB * b + x for x in range(SUB)]
            term = nt(w3[b], gather_hidden(hidden, starts, sizes.rows, two.shape[1]))
            total = term if total is None else total + term
        rest = jnp.zeros((total.shape[0], LANES - sizes.rows), F32)
        for x in range(SUB):
            piece = total[:, x * sizes.rows : (x + 1) * sizes.rows]
            turned[pl.ds(x, total.shape[0], stride=SUB), :] = jnp.concatenate([piece, rest], axis=1)
        for s in range(z):
            yz = [turned[(g * z + s) * SUB : (g * z + s + 1) * SUB, : sizes.rows] + b3[g] for g in range(3)]
            here = slice(start, start + SUB)
            out_ref[0, s, here, :] = yz[0]
            out_ref[1, s, here, :] = 0.5 * (xy_ref[0, s, here, :] + yz[1])
            out_ref[2, s, here, :] = xy_ref[1, s, here, :]
            out_ref[3, s, here, :] = 0.5 * (xy_ref[2, s, here, :] + yz[2])


def call(kernel, name, outs, args, scratch=(), flops=0):
    single = not isinstance(outs, list)
    shapes = [jax.ShapeDtypeStruct(shape, kind) for shape, kind in ([outs] if single else outs)]
    return pl.pallas_call(
        kernel,
        name=name,
        out_shape=shapes[0] if single else shapes,
        scratch_shapes=scratch,
        compiler_params=pltpu.CompilerParams(vmem_limit_bytes=LIMIT),
        cost_estimate=pl.CostEstimate(flops=flops, bytes_accessed=1 << 20, transcendentals=0),
    )(*args)


def local(image, first_kernel, first_bias, middle_kernel, middle_bias, last_kernel, last_bias):
    slices, rows, cols = image.shape
    channels, outputs = first_kernel.shape[2], last_kernel.shape[2]
    sizes = Sizes(slices, rows, cols, channels, outputs, lax.axis_size("slab"), lax.axis_size("row"))
    t = image.transpose(0, 2, 1)
    even, odd = swap_rows(t, 0), swap_rows(t, 1)
    own, *weights = call(
        functools.partial(prepare_kernel, sizes),
        "prepare",
        [(t.shape, BF16), *sizes.weight_shapes()],
        (
            t,
            first_kernel.reshape(3, 3, channels),
            first_bias.reshape(1, channels),
            middle_kernel,
            middle_bias.reshape(1, channels),
            last_kernel,
            last_bias.reshape(1, outputs),
        ),
        flops=1 << 20,
    )
    wide = rows + 6
    e = call(extend_kernel, "extend", ((slices, cols, wide), BF16), (own, even, odd))
    even, odd = swap_slabs(e, 0), swap_slabs(e, 1)
    lanes = max(kind[2][1] for kind in sizes.kinds) * channels
    xy_hidden = pltpu.VMEM(((sizes.span + 2) * SUB, LANES), F32)
    yz_hidden = pltpu.VMEM(((rows + 2) * SUB, LANES), F32)
    xy = call(
        functools.partial(xy_kernel, sizes),
        "xy",
        ((outputs, slices, cols, rows), F32),
        (e, *weights[5:]),
        [xy_hidden] * pl.cdiv(lanes, LANES),
        flops=1 << 28,
    )
    flows = call(
        functools.partial(yz_kernel, sizes),
        "yz",
        ((outputs + 1, slices, cols, rows), F32),
        (e, even, odd, xy, *weights[:5], weights[-1]),
        [pltpu.VMEM((outputs * slices * SUB, LANES), F32)]
        + [yz_hidden] * pl.cdiv((slices + 2) * channels, LANES),
        flops=1 << 28,
    )
    return flows.transpose(0, 1, 3, 2)


def solution(mesh):
    placed = (P("slab", "row", None), P(), P(), P(), P(), P(), P())
    return jax.shard_map(
        local, mesh=mesh, in_specs=placed, out_specs=P(None, "slab", "row", None), check_vma=False
    )
```

```python
import functools

import jax
import jax.numpy as jnp
from jax import lax
from jax.experimental import pallas as pl
from jax.experimental.pallas import tpu as pltpu
from jax.sharding import PartitionSpec as P

SUB = 8
LANES = 128
NEVER = -3.0e38
LIMIT = 12 << 20
F32 = jnp.float32
BF16 = jnp.bfloat16


def matching(count, parity):
    partner = {}
    for left in range(parity, count - 1, 2):
        partner[left] = left + 1
        partner[left + 1] = left
    return partner


def swap_rows(values, parity):
    count = lax.axis_size("row")
    partner = matching(count, parity)
    ends = [i for i in range(count) if i not in partner]
    for here, there in zip(ends, reversed(ends)):
        partner[here] = there
    return lax.ppermute(values, "row", sorted(partner.items()))


def swap_slabs(values, parity):
    slabs, rows = lax.axis_size("slab"), lax.axis_size("row")
    partner = matching(slabs, parity)
    across = matching(rows, 0)
    pairs = []
    for s in range(slabs):
        for r in range(rows):
            there = (partner[s], r) if s in partner else (s, across.get(r, r))
            pairs.append((s * rows + r, there[0] * rows + there[1]))
    return lax.ppermute(values, ("slab", "row"), pairs)


def before_and_after(even, odd, axis):
    here, count = lax.axis_index(axis), lax.axis_size(axis)
    low = here % 2 == 0
    before = jnp.where(low, odd, even)
    after = jnp.where(low, even, odd)
    before = jnp.where(here > 0, before, jnp.zeros_like(before))
    after = jnp.where(here < count - 1, after, jnp.zeros_like(after))
    return before, after


def tile_lanes(row, count):
    return jnp.concatenate([row] * count, axis=1)


def iota(shape, dim):
    return lax.broadcasted_iota(jnp.int32, shape, dim)


def nn(left, right):
    return lax.dot_general(left, right, (((1,), (0,)), ((), ())), preferred_element_type=F32)


def nt(left, right):
    return lax.dot_general(left, right, (((1,), (1,)), ((), ())), preferred_element_type=F32)


def keep_hidden(scratch, values):
    for i in range(0, values.shape[1], LANES):
        piece = values[:, i : i + LANES]
        scratch[i // LANES][:, : piece.shape[1]] = piece


def gather_hidden(scratch, starts, count, lanes):
    columns = []
    for i in range(0, lanes, LANES):
        parts = [scratch[i // LANES][pl.ds(start, count, stride=SUB), :] for start in starts]
        columns.append(jnp.concatenate(parts, axis=0).astype(BF16)[:, : lanes - i])
    return jnp.concatenate(columns, axis=1)


class Sizes:
    def __init__(self, slices, rows, cols, channels, outputs, slabs, parts):
        self.slices, self.rows, self.cols = slices, rows, cols
        self.channels, self.outputs = channels, outputs
        self.slabs, self.parts = slabs, parts
        assert slices >= 3 and SUB % slices == 0
        self.halves = SUB // slices
        assert rows % self.halves == 0 and cols % SUB == 0
        self.span = rows // self.halves
        self.chunks = []
        self.kinds = []
        for start in range(0, cols, SUB):
            ranges = []
            for reach in (3, 2, 1, 0):
                low = max(0, start - reach)
                ranges.append((low - start, min(cols, start + SUB + reach) - low))
            kind = tuple(ranges)
            if kind not in self.kinds:
                self.kinds.append(kind)
            self.chunks.append((start, self.kinds.index(kind)))

    def weight_shapes(self):
        c, z = self.channels, self.slices
        shapes = [
            ((3, 3 * z * SUB, (z + 4) * c), BF16),
            ((3, (z + 2) * c, (z + 4) * c), BF16),
            ((3, self.outputs * z, (z + 2) * c), BF16),
            ((1, (z + 4) * c), F32),
            ((1, (z + 2) * c), F32),
        ]
        for image, one, two, _ in self.kinds:
            shapes += [
                ((3, z * image[1], one[1] * c), BF16),
                ((3, two[1] * c, one[1] * c), BF16),
                ((3, self.outputs * SUB, two[1] * c), BF16),
                ((1, one[1] * c), F32),
                ((1, two[1] * c), F32),
            ]
        return shapes + [((self.outputs, SUB, self.rows), F32)]


def banded(blocks, out_count, in_count, offset):
    zero = jnp.zeros_like(blocks[0])
    lines = []
    for out in range(out_count):
        line = []
        for inner in range(in_count):
            tap = inner - out + offset
            line.append(blocks[tap] if 0 <= tap < 3 else zero)
        lines.append(jnp.concatenate(line, axis=1))
    return jnp.concatenate(lines, axis=0)


def spread(rows_of, tap_of, shape, lines):
    total = jnp.zeros(shape, F32)
    for (group, tap), line in lines.items():
        here = tap_of == tap
        if rows_of is not None:
            here = here & (rows_of == group)
        total = jnp.where(here, line, total)
    return total.astype(BF16)


def prepare_kernel(sizes, *refs):
    count = 7
    arguments, outs, held, sems = refs[:count], refs[count:-count], refs[-count:-1], refs[-1]
    t_out, *outs = outs
    copies = [
        pltpu.make_async_copy(here, there, sems.at[i])
        for i, (here, there) in enumerate(zip(arguments, (t_out, *held)))
    ]
    for copy in copies:
        copy.start()
    for copy in copies:
        copy.wait()
    c, z, n_out = sizes.channels, sizes.slices, sizes.outputs
    k1_ref, b1_ref, k2_ref, b2_ref, k3_ref, b3_ref = held
    k1 = k1_ref[...].astype(F32)
    k3 = k3_ref[...].astype(F32)
    b1, b2 = b1_ref[...], b2_ref[...]

    def first(shape, tap_of, tap_index):
        count = shape[1] // c
        lines = {(0, t): tile_lanes(k1[tap_index(t)[0], tap_index(t)[1]][None, :], count) for t in range(3)}
        return spread(None, tap_of, shape, lines)

    def last(shape, group_of, tap_of, tap_index):
        count = shape[1] // c
        lines = {}
        for g in range(n_out):
            for t in range(3):
                a, b = tap_index(t)
                lines[g, t] = tile_lanes(k3[a, b, g][None, :], count)
        return spread(group_of, tap_of, shape, lines)

    w1, w2, w3, c1, c2 = outs[:5]
    for b in range(3):
        shape = w1.shape[1:]
        tap = iota(shape, 0) // SUB - iota(shape, 1) // c + (3 - z)
        w1[b] = first(shape, tap, lambda t, b=b: (t, b))
        w2[b] = banded([k2_ref[a, b] for a in range(3)], z + 2, z + 4, 0)
        shape = w3.shape[1:]
        row = iota(shape, 0)
        w3[b] = last(shape, row // z, iota(shape, 1) // c - row % z, lambda t, b=b: (t, b))
    base = lax.axis_index("slab") * z
    for ref, bias, reach in ((c1, b1, 2), (c2, b2, 1)):
        where = base + iota(ref.shape, 1) // c - reach
        inside = (where >= 0) & (where < sizes.slabs * z)
        ref[...] = jnp.where(inside, tile_lanes(bias, ref.shape[1] // c), NEVER)

    for index, (image, one, two, out) in enumerate(sizes.kinds):
        w1, w2, w3, c1, c2 = outs[5 + 5 * index : 10 + 5 * index]
        for a in range(3):
            shape = w1.shape[1:]
            tap = iota(shape, 0) % image[1] + image[0] - iota(shape, 1) // c - one[0] + 1
            w1[a] = first(shape, tap, lambda t, a=a: (a, t))
            w2[a] = banded([k2_ref[a, b] for b in range(3)], two[1], one[1], one[0] - two[0] + 1)
            shape = w3.shape[1:]
            row = iota(shape, 0)
            tap = iota(shape, 1) // c + two[0] - row % SUB - out[0] + 1
            w3[a] = last(shape, row // SUB, tap, lambda t, a=a: (a, t))
        c1[...] = tile_lanes(b1, one[1])
        c2[...] = tile_lanes(b2, two[1])
    for g in range(n_out):
        outs[-1][g] = jnp.broadcast_to(b3_ref[0:1, g : g + 1], (SUB, sizes.rows))


def extend_kernel(own_ref, even_ref, odd_ref, out_ref):
    rows = own_ref.shape[2]
    before, after = before_and_after(even_ref[...], odd_ref[...], "row")
    out_ref[...] = jnp.concatenate([before[:, :, rows - 3 :], own_ref[...], after[:, :, :3]], axis=2)


def zero_groups(values, count, low, high):
    edge = count * SUB
    top, middle, bottom = values[:edge], values[edge:-edge], values[-edge:]
    if low.ndim:
        low, high = low[:edge], high[:edge]
    return jnp.concatenate([jnp.where(low, 0.0, top), middle, jnp.where(high, 0.0, bottom)], axis=0)


def taps(values, count):
    low, high = values.astype(BF16), values[SUB:].astype(BF16)
    return [low[:count], high[:count], low[2 * SUB : 2 * SUB + count]]


def hidden_layers(picked, groups, w1, w2, c1, c2, low, high):
    n1, n2 = (groups - 2) * SUB, (groups - 4) * SUB
    one = sum(nn(tap, w1[i]) for i, tap in enumerate(taps(picked, n1)))
    one = zero_groups(jnp.maximum(one + c1[...], 0.0), 2, low, high)
    two = sum(nt(tap, w2[i]) for i, tap in enumerate(taps(one, n2)))
    return zero_groups(jnp.maximum(two + c2[...], 0.0), 1, low, high)


def xy_kernel(sizes, e_ref, *refs):
    count = sum(1 for _ in sizes.kinds) * 5
    weights, (b3, out_ref, *hidden) = refs[:count], refs[count:]
    z, span = sizes.slices, sizes.span
    wide = sizes.rows + 6
    groups = span + 6
    row = lax.axis_index("row")
    half = iota((2 * SUB, 1), 0) % SUB // z
    low = (row == 0) & (half == 0)
    high = (row == sizes.parts - 1) & (half == sizes.halves - 1)
    shape = (groups * SUB, wide)
    wanted = iota(shape, 0) // SUB + iota(shape, 0) % SUB // z * span
    select = jnp.where(iota(shape, 1) == wanted, 1.0, 0.0).astype(BF16)
    for start, index in sizes.chunks:
        image = sizes.kinds[index][0]
        w1, w2, w3, c1, c2 = weights[5 * index : 5 * index + 5]
        low_col = start + image[0]
        e = e_ref[:, low_col : low_col + image[1], :].reshape(z * image[1], wide)
        picked = nt(select, e)
        same = iota(picked.shape, 1) // image[1] == iota(picked.shape, 0) % z
        picked = jnp.where(same, picked, 0.0)
        second = hidden_layers(picked, groups, w1, w2, c1, c2, low, high)
        keep_hidden(hidden, second)
        total = None
        for a in range(3):
            starts = [SUB * a + h * z + s for s in range(z) for h in range(sizes.halves)]
            term = nt(w3[a], gather_hidden(hidden, starts, span, second.shape[1]))
            total = term if total is None else total + term
        for g in range(sizes.outputs):
            for s in range(z):
                piece = total[g * SUB : (g + 1) * SUB, s * sizes.rows : (s + 1) * sizes.rows]
                out_ref[g, s, start : start + SUB, :] = piece + b3[g]


def yz_kernel(sizes, e_ref, even_ref, odd_ref, xy_ref, w1, w2, w3, c1, c2, b3, out_ref, turned, *hidden):
    z = sizes.slices
    wide = sizes.rows + 6
    groups = sizes.rows + 6
    row = lax.axis_index("row")
    low, high = row == 0, row == sizes.parts - 1
    before, after = before_and_after(even_ref[...], odd_ref[...], "slab")
    block = jnp.concatenate([before, e_ref[...], after], axis=0)
    shape = (groups * SUB, wide)
    select = jnp.where(iota(shape, 1) == iota(shape, 0) // SUB, 1.0, 0.0).astype(BF16)
    for start in range(0, sizes.cols, SUB):
        e = block[:, start : start + SUB, :].reshape(3 * z * SUB, wide)
        picked = nt(select, e)
        same = iota(picked.shape, 1) % SUB == iota(picked.shape, 0) % SUB
        picked = jnp.where(same, picked, 0.0)
        two = hidden_layers(picked, groups, w1, w2, c1, c2, low, high)
        keep_hidden(hidden, two)
        total = None
        for b in range(3):
            starts = [SUB * b + x for x in range(SUB)]
            term = nt(w3[b], gather_hidden(hidden, starts, sizes.rows, two.shape[1]))
            total = term if total is None else total + term
        rest = jnp.zeros((total.shape[0], LANES - sizes.rows), F32)
        for x in range(SUB):
            piece = total[:, x * sizes.rows : (x + 1) * sizes.rows]
            turned[pl.ds(x, total.shape[0], stride=SUB), :] = jnp.concatenate([piece, rest], axis=1)
        for s in range(z):
            yz = [turned[(g * z + s) * SUB : (g * z + s + 1) * SUB, : sizes.rows] + b3[g] for g in range(3)]
            here = slice(start, start + SUB)
            out_ref[0, s, here, :] = yz[0]
            out_ref[1, s, here, :] = 0.5 * (xy_ref[0, s, here, :] + yz[1])
            out_ref[2, s, here, :] = xy_ref[1, s, here, :]
            out_ref[3, s, here, :] = 0.5 * (xy_ref[2, s, here, :] + yz[2])


def call(kernel, name, outs, args, scratch=(), flops=0, space=pltpu.VMEM):
    single = not isinstance(outs, list)
    shapes = [jax.ShapeDtypeStruct(shape, kind) for shape, kind in ([outs] if single else outs)]
    return pl.pallas_call(
        kernel,
        name=name,
        out_shape=shapes[0] if single else shapes,
        in_specs=[pl.BlockSpec(memory_space=space)] * len(args),
        scratch_shapes=scratch,
        compiler_params=pltpu.CompilerParams(vmem_limit_bytes=LIMIT),
        cost_estimate=pl.CostEstimate(flops=flops, bytes_accessed=1 << 20, transcendentals=0),
    )(*args)


def local(image, first_kernel, first_bias, middle_kernel, middle_bias, last_kernel, last_bias):
    slices, rows, cols = image.shape
    channels, outputs = first_kernel.shape[2], last_kernel.shape[2]
    sizes = Sizes(slices, rows, cols, channels, outputs, lax.axis_size("slab"), lax.axis_size("row"))
    t = image.transpose(0, 2, 1)
    even, odd = swap_rows(t, 0), swap_rows(t, 1)
    parameters = (
        first_kernel.reshape(3, 3, channels),
        first_bias.reshape(1, channels),
        middle_kernel,
        middle_bias.reshape(1, channels),
        last_kernel,
        last_bias.reshape(1, outputs),
    )
    own, *weights = call(
        functools.partial(prepare_kernel, sizes),
        "prepare",
        [(t.shape, BF16), *sizes.weight_shapes()],
        [pltpu.with_memory_space_constraint(p, pltpu.HBM) for p in (t, *parameters)],
        [pltpu.VMEM(p.shape, p.dtype) for p in parameters] + [pltpu.SemaphoreType.DMA((7,))],
        flops=1 << 20,
        space=pltpu.HBM,
    )
    wide = rows + 6
    e = call(extend_kernel, "extend", ((slices, cols, wide), BF16), (own, even, odd))
    even, odd = swap_slabs(e, 0), swap_slabs(e, 1)
    lanes = max(kind[2][1] for kind in sizes.kinds) * channels
    xy_hidden = pltpu.VMEM(((sizes.span + 2) * SUB, LANES), F32)
    yz_hidden = pltpu.VMEM(((rows + 2) * SUB, LANES), F32)
    xy = call(
        functools.partial(xy_kernel, sizes),
        "xy",
        ((outputs, slices, cols, rows), F32),
        (e, *weights[5:]),
        [xy_hidden] * pl.cdiv(lanes, LANES),
        flops=1 << 28,
    )
    flows = call(
        functools.partial(yz_kernel, sizes),
        "yz",
        ((outputs + 1, slices, cols, rows), F32),
        (e, even, odd, xy, *weights[:5], weights[-1]),
        [pltpu.VMEM((outputs * slices * SUB, LANES), F32)]
        + [yz_hidden] * pl.cdiv((slices + 2) * channels, LANES),
        flops=1 << 28,
    )
    return flows.transpose(0, 1, 3, 2)


def solution(mesh):
    placed = (P("slab", "row", None), P(), P(), P(), P(), P(), P())
    return jax.shard_map(
        local, mesh=mesh, in_specs=placed, out_specs=P(None, "slab", "row", None), check_vma=False
    )
```

```python
import functools

import jax
import jax.numpy as jnp
from jax import lax
from jax.experimental import pallas as pl
from jax.experimental.pallas import tpu as pltpu
from jax.sharding import PartitionSpec as P

SUB = 8
LANES = 128
NEVER = -3.0e38
LIMIT = 12 << 20
F32 = jnp.float32
BF16 = jnp.bfloat16


def matching(count, parity):
    partner = {}
    for left in range(parity, count - 1, 2):
        partner[left] = left + 1
        partner[left + 1] = left
    return partner


def swap_rows(values, parity):
    count = lax.axis_size("row")
    partner = matching(count, parity)
    ends = [i for i in range(count) if i not in partner]
    for here, there in zip(ends, reversed(ends)):
        partner[here] = there
    return lax.ppermute(values, "row", sorted(partner.items()))


def slab_rounds(slabs):
    borders = range(slabs - 1)
    return [borders[:1], borders[1::2], borders[2::2]]


def swap_slabs(values, borders):
    slabs, rows = lax.axis_size("slab"), lax.axis_size("row")
    partner = {}
    for border in borders:
        partner[border], partner[border + 1] = border + 1, border
    across = matching(rows, 0)
    pairs = []
    for s in range(slabs):
        for r in range(rows):
            there = (partner[s], r) if s in partner else (s, across.get(r, r))
            pairs.append((s * rows + r, there[0] * rows + there[1]))
    return lax.ppermute(values, ("slab", "row"), pairs)


def before_and_after(even, odd, axis):
    here, count = lax.axis_index(axis), lax.axis_size(axis)
    low = here % 2 == 0
    before = jnp.where(low, odd, even)
    after = jnp.where(low, even, odd)
    before = jnp.where(here > 0, before, jnp.zeros_like(before))
    after = jnp.where(here < count - 1, after, jnp.zeros_like(after))
    return before, after


def tile_lanes(row, count):
    return jnp.concatenate([row] * count, axis=1)


def iota(shape, dim):
    return lax.broadcasted_iota(jnp.int32, shape, dim)


def nn(left, right):
    return lax.dot_general(left, right, (((1,), (0,)), ((), ())), preferred_element_type=F32)


def nt(left, right):
    return lax.dot_general(left, right, (((1,), (1,)), ((), ())), preferred_element_type=F32)


def keep_hidden(scratch, values):
    for i in range(0, values.shape[1], LANES):
        piece = values[:, i : i + LANES]
        scratch[i // LANES][: piece.shape[0], : piece.shape[1]] = piece


def gather_hidden(scratch, runs, lanes):
    columns = []
    for i in range(0, lanes, LANES):
        parts = [scratch[i // LANES][pl.ds(start, count, stride=SUB), :] for start, count in runs]
        columns.append(jnp.concatenate(parts, axis=0).astype(BF16)[:, : lanes - i])
    return jnp.concatenate(columns, axis=1)


def last_layer(w3, hidden):
    every = nt(w3[...], hidden)
    count, lanes = every.shape[0] // 3, every.shape[1] - SUB
    return sum(every[i * count : (i + 1) * count, i : i + lanes] for i in range(3))


class Sizes:
    def __init__(self, slices, rows, cols, channels, outputs, slabs, parts):
        self.slices, self.rows, self.cols = slices, rows, cols
        self.channels, self.outputs = channels, outputs
        self.slabs, self.parts = slabs, parts
        assert slices >= 3 and SUB % slices == 0
        self.halves = SUB // slices
        assert rows % self.halves == 0 and cols % SUB == 0
        self.span = rows // self.halves
        self.padded = -(-outputs * slices // SUB) * SUB
        self.slot = rows + SUB
        self.chunks = []
        self.kinds = []
        for start in range(0, cols, SUB):
            ranges = []
            for reach in (3, 2, 1, 0):
                low = max(0, start - reach)
                ranges.append((low - start, min(cols, start + SUB + reach) - low))
            kind = tuple(ranges)
            if kind not in self.kinds:
                self.kinds.append(kind)
            self.chunks.append((start, self.kinds.index(kind)))

    def weight_shapes(self):
        c, z = self.channels, self.slices
        shapes = [
            ((3 * (z + 6) * SUB, (z + 4) * c), BF16),
            ((3, (z + 4) * c, (z + 2) * c), BF16),
            ((3 * self.padded, (z + 2) * c), BF16),
            ((1, (z + 4) * c), F32),
            ((1, (z + 2) * c), F32),
        ]
        for image, one, two, _ in self.kinds:
            shapes += [
                ((3 * z * image[1], one[1] * c), BF16),
                ((3, one[1] * c, two[1] * c), BF16),
                ((3 * self.outputs * SUB, two[1] * c), BF16),
                ((1, one[1] * c), F32),
                ((1, two[1] * c), F32),
            ]
        return shapes + [((self.outputs, SUB, self.rows), F32)]


def banded(blocks, out_count, in_count, offset):
    zero = jnp.zeros_like(blocks[0])
    lines = []
    for inner in range(in_count):
        line = []
        for out in range(out_count):
            tap = inner - out + offset
            line.append(blocks[tap] if 0 <= tap < 3 else zero)
        lines.append(jnp.concatenate(line, axis=1))
    return jnp.concatenate(lines, axis=0)


def spread(tap_of, group_of, shape, lines):
    total = jnp.zeros(shape, F32)
    for (group, tap), line in lines.items():
        total = jnp.where((tap_of == tap) & (group_of == group), line, total)
    return total.astype(BF16)


def prepare_kernel(sizes, *refs):
    count = 7
    arguments, outs, held, sems = refs[:count], refs[count:-count], refs[-count:-1], refs[-1]
    t_out, *outs = outs
    copies = [
        pltpu.make_async_copy(here, there, sems.at[i])
        for i, (here, there) in enumerate(zip(arguments, (t_out, *held)))
    ]
    for copy in copies:
        copy.start()
    for copy in copies:
        copy.wait()
    c, z, n_out = sizes.channels, sizes.slices, sizes.outputs
    k1_ref, b1_ref, k2_ref, b2_ref, k3_ref, b3_ref = held
    k1 = k1_ref[...].astype(F32)
    k3 = k3_ref[...].astype(F32)
    b1, b2 = b1_ref[...], b2_ref[...]

    k2 = [[k2_ref[a, b].astype(F32).T.astype(BF16) for b in range(3)] for a in range(3)]

    def first(ref, tap_of, tap_index):
        rows, lanes = ref.shape[0] // 3, ref.shape[1]
        for shift in range(3):
            lines = {(0, t): tile_lanes(k1[tap_index(shift, t)][None, :], lanes // c) for t in range(3)}
            ref[shift * rows : (shift + 1) * rows, :] = spread(tap_of, 0, (rows, lanes), lines)

    def last(shape, group_of, tap_of, tap_index, shift):
        lines = {
            (g, t): tile_lanes(k3[tap_index(shift, t)][g][None, :], shape[1] // c)
            for g in range(n_out)
            for t in range(3)
        }
        return spread(tap_of, group_of, shape, lines)

    def along_z(shift, t):
        return t, shift

    def along_x(shift, t):
        return shift, t

    w1, w2, w3, c1, c2 = outs[:5]
    shape = (w1.shape[0] // 3, w1.shape[1])
    first(w1, iota(shape, 0) // SUB - iota(shape, 1) // c, along_z)
    shape = (w3.shape[0] // 3, w3.shape[1])
    row = iota(shape, 0)
    for b in range(3):
        w2[b] = banded([k2[a][b] for a in range(3)], z + 2, z + 4, 0)
        w3[b * shape[0] : (b + 1) * shape[0], :] = last(
            shape, row // z, iota(shape, 1) // c - row % z, along_z, b
        )
    base = lax.axis_index("slab") * z
    for ref, bias, reach in ((c1, b1, 2), (c2, b2, 1)):
        where = base + iota(ref.shape, 1) // c - reach
        inside = (where >= 0) & (where < sizes.slabs * z)
        ref[...] = jnp.where(inside, tile_lanes(bias, ref.shape[1] // c), NEVER)

    for index, (image, one, two, out) in enumerate(sizes.kinds):
        w1, w2, w3, c1, c2 = outs[5 + 5 * index : 10 + 5 * index]
        shape = (w1.shape[0] // 3, w1.shape[1])
        first(w1, iota(shape, 0) % image[1] + image[0] - iota(shape, 1) // c - one[0] + 1, along_x)
        shape = (w3.shape[0] // 3, w3.shape[1])
        row = iota(shape, 0)
        tap = iota(shape, 1) // c + two[0] - row % SUB - out[0] + 1
        for a in range(3):
            w2[a] = banded([k2[a][b] for b in range(3)], two[1], one[1], one[0] - two[0] + 1)
            w3[a * shape[0] : (a + 1) * shape[0], :] = last(shape, row // SUB, tap, along_x, a)
        c1[...] = tile_lanes(b1, one[1])
        c2[...] = tile_lanes(b2, two[1])
    for g in range(n_out):
        outs[-1][g] = jnp.broadcast_to(b3_ref[0:1, g : g + 1], (SUB, sizes.rows))


def extend_kernel(own_ref, even_ref, odd_ref, out_ref):
    rows = own_ref.shape[2]
    before, after = before_and_after(even_ref[...], odd_ref[...], "row")
    out_ref[...] = jnp.concatenate([before[:, :, rows - 3 :], own_ref[...], after[:, :, :3]], axis=2)


def zero_groups(values, count, low, high):
    edge = count * SUB
    top, middle, bottom = values[:edge], values[edge:-edge], values[-edge:]
    if low.ndim:
        low, high = low[:edge], high[:edge]
    return jnp.concatenate([jnp.where(low, 0.0, top), middle, jnp.where(high, 0.0, bottom)], axis=0)


def taps(values, count):
    low, high = values.astype(BF16), values[SUB:].astype(BF16)
    return [low[:count], high[:count], low[2 * SUB : 2 * SUB + count]]


def pick(select, e):
    count = select.shape[1]
    return nt(select, jnp.concatenate([e[:, shift : shift + count] for shift in range(3)], axis=0))


def hidden_layers(picked, w1, w2, c1, c2, low, high):
    n2 = picked.shape[0] - 2 * SUB
    one = nn(picked.astype(BF16), w1[...])
    one = zero_groups(jnp.maximum(one + c1[...], 0.0), 2, low, high)
    two = sum(nn(tap, w2[i]) for i, tap in enumerate(taps(one, n2)))
    return zero_groups(jnp.maximum(two + c2[...], 0.0), 1, low, high)


def xy_kernel(sizes, e_ref, *refs):
    count = sum(1 for _ in sizes.kinds) * 5
    weights, (b3, out_ref, *hidden) = refs[:count], refs[count:]
    z, span = sizes.slices, sizes.span
    wide = sizes.rows + 6
    row = lax.axis_index("row")
    half = iota((2 * SUB, 1), 0) % SUB // z
    low = (row == 0) & (half == 0)
    high = (row == sizes.parts - 1) & (half == sizes.halves - 1)
    shape = ((span + 4) * SUB, sizes.rows + 4)
    wanted = iota(shape, 0) // SUB + iota(shape, 0) % SUB // z * span
    select = jnp.where(iota(shape, 1) == wanted, 1.0, 0.0).astype(BF16)
    for start, index in sizes.chunks:
        image = sizes.kinds[index][0]
        w1, w2, w3, c1, c2 = weights[5 * index : 5 * index + 5]
        low_col = start + image[0]
        e = e_ref[:, low_col : low_col + image[1], :].reshape(z * image[1], wide)
        picked = pick(select, e)
        same = iota(picked.shape, 1) // image[1] % z == iota(picked.shape, 0) % z
        picked = jnp.where(same, picked, 0.0)
        second = hidden_layers(picked, w1, w2, c1, c2, low, high)
        keep_hidden(hidden, second)
        runs = [
            (h * z + s, span if h < sizes.halves - 1 else span + SUB)
            for s in range(z)
            for h in range(sizes.halves)
        ]
        total = last_layer(w3, gather_hidden(hidden, runs, second.shape[1]))
        for g in range(sizes.outputs):
            for s in range(z):
                piece = total[g * SUB : (g + 1) * SUB, s * sizes.slot : s * sizes.slot + sizes.rows]
                out_ref[g, s, start : start + SUB, :] = piece + b3[g]


def yz_kernel(sizes, e_ref, even_ref, odd_ref, first_ref, xy_ref, w1, w2, w3, c1, c2, b3, out_ref, turned, *hidden):
    z = sizes.slices
    wide = sizes.rows + 6
    row = lax.axis_index("row")
    low, high = row == 0, row == sizes.parts - 1
    slab = lax.axis_index("slab")
    even = jnp.where(slab < 2, first_ref[...], even_ref[...])
    before, after = before_and_after(even, odd_ref[...], "slab")
    block = jnp.concatenate([before[z - 3 :], e_ref[...], after[:3]], axis=0)
    shape = ((sizes.rows + 4) * SUB, sizes.rows + 4)
    select = jnp.where(iota(shape, 1) == iota(shape, 0) // SUB, 1.0, 0.0).astype(BF16)
    for start in range(0, sizes.cols, SUB):
        e = block[:, start : start + SUB, :].reshape((z + 6) * SUB, wide)
        picked = pick(select, e)
        same = iota(picked.shape, 1) % SUB == iota(picked.shape, 0) % SUB
        picked = jnp.where(same, picked, 0.0)
        two = hidden_layers(picked, w1, w2, c1, c2, low, high)
        keep_hidden(hidden, two)
        runs = [(x, sizes.slot) for x in range(SUB)]
        total = last_layer(w3, gather_hidden(hidden, runs, two.shape[1]))
        rest = jnp.zeros((total.shape[0], LANES - sizes.rows), F32)
        for x in range(SUB):
            piece = total[:, x * sizes.slot : x * sizes.slot + sizes.rows]
            turned[pl.ds(x, total.shape[0], stride=SUB), :] = jnp.concatenate([piece, rest], axis=1)
        for s in range(z):
            yz = [turned[(g * z + s) * SUB : (g * z + s + 1) * SUB, : sizes.rows] + b3[g] for g in range(3)]
            here = slice(start, start + SUB)
            out_ref[0, s, here, :] = yz[0]
            out_ref[1, s, here, :] = 0.5 * (xy_ref[0, s, here, :] + yz[1])
            out_ref[2, s, here, :] = xy_ref[1, s, here, :]
            out_ref[3, s, here, :] = 0.5 * (xy_ref[2, s, here, :] + yz[2])


def call(kernel, name, outs, args, scratch=(), flops=0, space=pltpu.VMEM):
    single = not isinstance(outs, list)
    shapes = [jax.ShapeDtypeStruct(shape, kind) for shape, kind in ([outs] if single else outs)]
    return pl.pallas_call(
        kernel,
        name=name,
        out_shape=shapes[0] if single else shapes,
        in_specs=[pl.BlockSpec(memory_space=space)] * len(args),
        scratch_shapes=scratch,
        compiler_params=pltpu.CompilerParams(vmem_limit_bytes=LIMIT),
        cost_estimate=pl.CostEstimate(flops=flops, bytes_accessed=1 << 20, transcendentals=0),
    )(*args)


def local(image, first_kernel, first_bias, middle_kernel, middle_bias, last_kernel, last_bias):
    slices, rows, cols = image.shape
    channels, outputs = first_kernel.shape[2], last_kernel.shape[2]
    sizes = Sizes(slices, rows, cols, channels, outputs, lax.axis_size("slab"), lax.axis_size("row"))
    t = image.transpose(0, 2, 1)
    even, odd = swap_rows(t, 0), swap_rows(t, 1)
    parameters = (
        first_kernel.reshape(3, 3, channels),
        first_bias.reshape(1, channels),
        middle_kernel,
        middle_bias.reshape(1, channels),
        last_kernel,
        last_bias.reshape(1, outputs),
    )
    own, *weights = call(
        functools.partial(prepare_kernel, sizes),
        "prepare",
        [(t.shape, BF16), *sizes.weight_shapes()],
        [pltpu.with_memory_space_constraint(p, pltpu.HBM) for p in (t, *parameters)],
        [pltpu.VMEM(p.shape, p.dtype) for p in parameters] + [pltpu.SemaphoreType.DMA((7,))],
        flops=1 << 20,
        space=pltpu.HBM,
    )
    wide = rows + 6
    e = call(extend_kernel, "extend", ((slices, cols, wide), BF16), (own, even, odd))
    swapped = [swap_slabs(e, borders) for borders in reversed(slab_rounds(sizes.slabs))]
    lanes = max(kind[2][1] for kind in sizes.kinds) * channels
    xy_hidden = pltpu.VMEM(((sizes.span + SUB) * SUB, LANES), F32)
    yz_hidden = pltpu.VMEM((sizes.slot * SUB, LANES), F32)
    xy = call(
        functools.partial(xy_kernel, sizes),
        "xy",
        ((outputs, slices, cols, rows), F32),
        (e, *weights[5:]),
        [xy_hidden] * pl.cdiv(lanes, LANES),
        flops=1 << 28,
    )
    flows = call(
        functools.partial(yz_kernel, sizes),
        "yz",
        ((outputs + 1, slices, cols, rows), F32),
        (e, *swapped, xy, *weights[:5], weights[-1]),
        [pltpu.VMEM((sizes.padded * SUB, LANES), F32)]
        + [yz_hidden] * pl.cdiv((slices + 2) * channels, LANES),
        flops=1 << 28,
    )
    return flows.transpose(0, 1, 3, 2)


def solution(mesh):
    placed = (P("slab", "row", None), P(), P(), P(), P(), P(), P())
    return jax.shard_map(
        local, mesh=mesh, in_specs=placed, out_specs=P(None, "slab", "row", None), check_vma=False
    )
```

```python
import functools

import jax
import jax.numpy as jnp
from jax import lax
from jax.experimental import pallas as pl
from jax.experimental.pallas import tpu as pltpu
from jax.sharding import PartitionSpec as P

SUB = 8
LANES = 128
SLOT = 64
YZ, XY = 6, 5
NEVER = -3.0e38
LIMIT = 12 << 20
F32 = jnp.float32
BF16 = jnp.bfloat16


def matching(count, parity):
    partner = {}
    for left in range(parity, count - 1, 2):
        partner[left] = left + 1
        partner[left + 1] = left
    return partner


def swap_rows(values, parity):
    count = lax.axis_size("row")
    partner = matching(count, parity)
    ends = [i for i in range(count) if i not in partner]
    for here, there in zip(ends, reversed(ends)):
        partner[here] = there
    return lax.ppermute(values, "row", sorted(partner.items()))


EARLY = 2


def slab_rounds(slabs, row):
    borders = list(range(slabs - 1))
    if row < EARLY:
        return [borders[:1] + borders[3::2], borders[1:2] + borders[4::2], borders[2:3]]
    return [borders[1::2], borders[::2], []]


def swap_slabs(values, turn_of):
    slabs, rows = lax.axis_size("slab"), lax.axis_size("row")
    across = matching(rows, 0)
    pairs = []
    for r in range(rows):
        partner = {}
        for border in slab_rounds(slabs, r)[turn_of]:
            partner[border], partner[border + 1] = border + 1, border
        for s in range(slabs):
            there = (partner[s], r) if s in partner else (s, across.get(r, r))
            pairs.append((s * rows + r, there[0] * rows + there[1]))
    return lax.ppermute(values, ("slab", "row"), sorted(pairs))


def before_and_after(even, odd, axis):
    here, count = lax.axis_index(axis), lax.axis_size(axis)
    low = here % 2 == 0
    before = jnp.where(low, odd, even)
    after = jnp.where(low, even, odd)
    before = jnp.where(here > 0, before, jnp.zeros_like(before))
    after = jnp.where(here < count - 1, after, jnp.zeros_like(after))
    return before, after


def tile_lanes(row, count):
    return jnp.concatenate([row] * count, axis=1)


def iota(shape, dim):
    return lax.broadcasted_iota(jnp.int32, shape, dim)


def nn(left, right):
    return lax.dot_general(left, right, (((1,), (0,)), ((), ())), preferred_element_type=F32)


def nt(left, right):
    return lax.dot_general(left, right, (((1,), (1,)), ((), ())), preferred_element_type=F32)


def keep_hidden(scratch, values):
    for i in range(0, values.shape[1], LANES):
        piece = values[:, i : i + LANES]
        scratch[i // LANES][: piece.shape[0], : piece.shape[1]] = piece


def gather_hidden(scratch, runs, lanes):
    columns = []
    for i in range(0, lanes, LANES):
        parts = [scratch[i // LANES][pl.ds(start, count, stride=SUB), :] for start, count in runs]
        columns.append(jnp.concatenate(parts, axis=0).astype(BF16)[:, : lanes - i])
    return jnp.concatenate(columns, axis=1)


def last_layer(w3, hidden):
    every = nt(w3[...], hidden)
    count, lanes = every.shape[0] // 3, every.shape[1] - SUB
    return sum(every[i * count : (i + 1) * count, i : i + lanes] for i in range(3))


class Sizes:
    def __init__(self, slices, rows, cols, channels, outputs, slabs, parts):
        self.slices, self.rows, self.cols = slices, rows, cols
        self.channels, self.outputs = channels, outputs
        self.slabs, self.parts = slabs, parts
        assert slices >= 3 and SUB % slices == 0 and rows + 6 <= SLOT
        self.halves = SUB // slices
        assert rows % self.halves == 0 and cols % SUB == 0
        self.span = rows // self.halves
        self.padded = -(-outputs * slices // SUB) * SUB
        self.slot = rows + SUB
        self.chunks = []
        self.kinds = []
        for start in range(0, cols, SUB):
            ranges = []
            for reach in (3, 2, 1, 0):
                low = max(0, start - reach)
                ranges.append((low - start, min(cols, start + SUB + reach) - low))
            kind = tuple(ranges)
            if kind not in self.kinds:
                self.kinds.append(kind)
            self.chunks.append((start, self.kinds.index(kind)))

    def weight_shapes(self):
        c, z = self.channels, self.slices
        shapes = [
            (((z + 4) * c, 3 * (z + 6) * SUB), BF16),
            ((3, (z + 2) * c, (z + 4) * c), BF16),
            ((3 * self.padded, (z + 2) * c), BF16),
            (((z + 4) * c, LANES), F32),
            (((z + 2) * c, LANES), F32),
            ((3 * (z + 6) * SUB, SUB * SLOT), BF16),
        ]
        for image, one, two, _ in self.kinds:
            shapes += [
                ((3 * z * image[1], one[1] * c), BF16),
                ((3, one[1] * c, two[1] * c), BF16),
                ((3 * self.outputs * SUB, two[1] * c), BF16),
                ((1, one[1] * c), F32),
                ((1, two[1] * c), F32),
            ]
        return shapes + [((self.outputs, SUB, self.rows), F32)]


def banded(blocks, row_count, lane_count, tap_of):
    zero = jnp.zeros_like(blocks[0])
    lines = []
    for row in range(row_count):
        line = [tap_of(row, lane) for lane in range(lane_count)]
        lines.append(jnp.concatenate([blocks[tap] if 0 <= tap < 3 else zero for tap in line], axis=1))
    return jnp.concatenate(lines, axis=0)


def spread(tap_of, group_of, shape, lines):
    total = jnp.zeros(shape, F32)
    for (group, tap), line in lines.items():
        total = jnp.where((tap_of == tap) & (group_of == group), line, total)
    return total


def prepare_kernel(sizes, *refs):
    count = 7
    arguments, outs, held, sems = refs[:count], refs[count:-count], refs[-count:-1], refs[-1]
    t_out, *outs = outs
    copies = [
        pltpu.make_async_copy(here, there, sems.at[i])
        for i, (here, there) in enumerate(zip(arguments, (t_out, *held)))
    ]
    for copy in copies:
        copy.start()
    for copy in copies:
        copy.wait()
    c, z, n_out = sizes.channels, sizes.slices, sizes.outputs
    k1_ref, b1_ref, k2_ref, b2_ref, k3_ref, b3_ref = held
    k1 = k1_ref[...].astype(F32)
    k3 = k3_ref[...].astype(F32)
    b1, b2 = b1_ref[...], b2_ref[...]

    k2 = [[k2_ref[a, b].astype(F32).T.astype(BF16) for b in range(3)] for a in range(3)]

    def first(shape, tap_of, tap_index):
        parts = []
        for shift in range(3):
            lines = {(0, t): tile_lanes(k1[tap_index(shift, t)][None, :], shape[1] // c) for t in range(3)}
            parts.append(spread(tap_of, 0, shape, lines))
        return jnp.concatenate(parts, axis=0)

    def last(shape, group_of, tap_of, tap_index, shift):
        lines = {
            (g, t): tile_lanes(k3[tap_index(shift, t)][g][None, :], shape[1] // c)
            for g in range(n_out)
            for t in range(3)
        }
        return spread(tap_of, group_of, shape, lines).astype(BF16)

    def along_z(shift, t):
        return t, shift

    def along_x(shift, t):
        return shift, t

    w1, w2, w3, c1, c2, mask = outs[:YZ]
    shape = (w1.shape[1] // 3, w1.shape[0])
    w1[...] = first(shape, iota(shape, 0) // SUB - iota(shape, 1) // c, along_z).T.astype(BF16)
    shape = (w3.shape[0] // 3, w3.shape[1])
    row = iota(shape, 0)
    for b in range(3):
        w2[b] = banded([k2_ref[a, b] for a in range(3)], z + 2, z + 4, lambda row, lane: lane - row)
        w3[b * shape[0] : (b + 1) * shape[0], :] = last(
            shape, row // z, iota(shape, 1) // c - row % z, along_z, b
        )
    base_z, base_y = lax.axis_index("slab") * z, lax.axis_index("row") * sizes.rows
    for ref, bias, reach in ((c1, b1, 2), (c2, b2, 1)):
        at_z = base_z + iota(ref.shape, 0) // c - reach
        at_y = base_y + iota(ref.shape, 1) % SLOT - reach
        inside = (at_z >= 0) & (at_z < sizes.slabs * z) & (at_y >= 0) & (at_y < sizes.parts * sizes.rows)
        column = jnp.broadcast_to(bias, (LANES, c)).T
        ref[...] = jnp.where(inside, jnp.concatenate([column] * (ref.shape[0] // c), axis=0), NEVER)
    mask[...] = jnp.where(iota(mask.shape, 0) % SUB == iota(mask.shape, 1) // SLOT, 1.0, 0.0).astype(BF16)

    for index, (image, one, two, out) in enumerate(sizes.kinds):
        w1, w2, w3, c1, c2 = outs[YZ + XY * index : YZ + XY * (index + 1)]
        shape = (w1.shape[0] // 3, w1.shape[1])
        tap = iota(shape, 0) % image[1] + image[0] - iota(shape, 1) // c - one[0] + 1
        w1[...] = first(shape, tap, along_x).astype(BF16)
        shape = (w3.shape[0] // 3, w3.shape[1])
        row = iota(shape, 0)
        tap = iota(shape, 1) // c + two[0] - row % SUB - out[0] + 1
        for a in range(3):
            w2[a] = banded(
                [k2[a][b] for b in range(3)],
                one[1],
                two[1],
                lambda row, lane, move=one[0] - two[0] + 1: row - lane + move,
            )
            w3[a * shape[0] : (a + 1) * shape[0], :] = last(shape, row // SUB, tap, along_x, a)
        c1[...] = tile_lanes(b1, one[1])
        c2[...] = tile_lanes(b2, two[1])
    for g in range(n_out):
        outs[-1][g] = jnp.broadcast_to(b3_ref[0:1, g : g + 1], (SUB, sizes.rows))


def extend_kernel(own_ref, even_ref, odd_ref, out_ref):
    rows = own_ref.shape[2]
    before, after = before_and_after(even_ref[...], odd_ref[...], "row")
    out_ref[...] = jnp.concatenate([before[:, :, rows - 3 :], own_ref[...], after[:, :, :3]], axis=2)


def zero_groups(values, count, low, high):
    edge = count * SUB
    top, middle, bottom = values[:edge], values[edge:-edge], values[-edge:]
    if low.ndim:
        low, high = low[:edge], high[:edge]
    return jnp.concatenate([jnp.where(low, 0.0, top), middle, jnp.where(high, 0.0, bottom)], axis=0)


def taps(values, count):
    low, high = values.astype(BF16), values[SUB:].astype(BF16)
    return [low[:count], high[:count], low[2 * SUB : 2 * SUB + count]]


def pick(select, e):
    count = select.shape[1]
    return nt(select, jnp.concatenate([e[:, shift : shift + count] for shift in range(3)], axis=0))


def hidden_layers(picked, w1, w2, c1, c2, low, high):
    n2 = picked.shape[0] - 2 * SUB
    one = nn(picked.astype(BF16), w1[...])
    one = zero_groups(jnp.maximum(one + c1[...], 0.0), 2, low, high)
    two = sum(nn(tap, w2[i]) for i, tap in enumerate(taps(one, n2)))
    return zero_groups(jnp.maximum(two + c2[...], 0.0), 1, low, high)


def xy_kernel(sizes, e_ref, *refs):
    count = XY * len(sizes.kinds)
    weights, (b3, out_ref, *hidden) = refs[:count], refs[count:]
    z, span = sizes.slices, sizes.span
    wide = sizes.rows + 6
    row = lax.axis_index("row")
    half = iota((2 * SUB, 1), 0) % SUB // z
    low = (row == 0) & (half == 0)
    high = (row == sizes.parts - 1) & (half == sizes.halves - 1)
    shape = ((span + 4) * SUB, sizes.rows + 4)
    wanted = iota(shape, 0) // SUB + iota(shape, 0) % SUB // z * span
    select = jnp.where(iota(shape, 1) == wanted, 1.0, 0.0).astype(BF16)
    for start, index in sizes.chunks:
        image = sizes.kinds[index][0]
        w1, w2, w3, c1, c2 = weights[XY * index : XY * (index + 1)]
        low_col = start + image[0]
        e = e_ref[:, low_col : low_col + image[1], :].reshape(z * image[1], wide)
        picked = pick(select, e)
        same = iota(picked.shape, 1) // image[1] % z == iota(picked.shape, 0) % z
        picked = jnp.where(same, picked, 0.0)
        second = hidden_layers(picked, w1, w2, c1, c2, low, high)
        keep_hidden(hidden, second)
        runs = [
            (h * z + s, span if h < sizes.halves - 1 else span + SUB)
            for s in range(z)
            for h in range(sizes.halves)
        ]
        total = last_layer(w3, gather_hidden(hidden, runs, second.shape[1]))
        for g in range(sizes.outputs):
            for s in range(z):
                piece = total[g * SUB : (g + 1) * SUB, s * sizes.slot : s * sizes.slot + sizes.rows]
                out_ref[g, s, start : start + SUB, :] = piece + b3[g]


def turn(values, count):
    if not count:
        return values
    tiles = [values[:, i : i + LANES] for i in range(0, values.shape[1], LANES)]
    tiles = [jnp.concatenate([tile[:, count:], tile[:, :count]], axis=1) for tile in tiles]
    return jnp.concatenate(tiles, axis=1)


def yz_kernel(sizes, e_ref, round_2, round_1, round_0, xy_ref, w1, w2, w3, c1, c2, mask, b3, out_ref, turned):
    z = sizes.slices
    wide = sizes.rows + 6
    slab = lax.axis_index("slab")
    early = lax.axis_index("row") < EARLY
    swapped = [ref[...] for ref in (round_0, round_1, round_2)]
    even = jnp.where(early & (slab < 2), swapped[0], swapped[1])
    even = jnp.where(early & (slab >= 2) & (slab < 4), swapped[2], even)
    odd = jnp.where(early & (slab >= 1) & (slab < 3), swapped[1], swapped[0])
    before, after = before_and_after(even, odd, "slab")
    block = jnp.concatenate([before[z - 3 :], e_ref[...], after[:3]], axis=0)
    per_tile = LANES // SLOT
    for start in range(0, sizes.cols, SUB):
        e = block[:, start : start + SUB, :].reshape((z + 6) * SUB, wide)
        shifted = jnp.concatenate([e[:, shift : shift + wide - 2] for shift in range(3)], axis=0)
        rest = jnp.zeros((shifted.shape[0], SLOT - wide + 2), BF16)
        tile = jnp.concatenate([shifted, rest] * per_tile, axis=1)
        count = SUB // per_tile
        picked = jnp.concatenate([tile] * count, axis=1) * mask[...]
        one = nn(w1[...], picked) + tile_lanes(c1[...], count)
        one = jnp.maximum(one, 0.0).astype(BF16)
        two = sum(nn(w2[b], turn(one, b)) for b in range(3)) + tile_lanes(c2[...], count)
        two = jnp.maximum(two, 0.0).astype(BF16)
        every = nn(w3[...], two)
        total = sum(turn(every[b * sizes.padded : (b + 1) * sizes.padded], b) for b in range(3))
        for x in range(SUB):
            tile = total[:, x // per_tile * LANES : (x // per_tile + 1) * LANES]
            turned[pl.ds(x, total.shape[0], stride=SUB), :] = turn(tile, x % per_tile * SLOT)
        for s in range(z):
            yz = [turned[(g * z + s) * SUB : (g * z + s + 1) * SUB, : sizes.rows] + b3[g] for g in range(3)]
            here = slice(start, start + SUB)
            out_ref[0, s, here, :] = yz[0]
            out_ref[1, s, here, :] = 0.5 * (xy_ref[0, s, here, :] + yz[1])
            out_ref[2, s, here, :] = xy_ref[1, s, here, :]
            out_ref[3, s, here, :] = 0.5 * (xy_ref[2, s, here, :] + yz[2])


def call(kernel, name, outs, args, scratch=(), flops=0, space=pltpu.VMEM):
    single = not isinstance(outs, list)
    shapes = [jax.ShapeDtypeStruct(shape, kind) for shape, kind in ([outs] if single else outs)]
    return pl.pallas_call(
        kernel,
        name=name,
        out_shape=shapes[0] if single else shapes,
        in_specs=[pl.BlockSpec(memory_space=space)] * len(args),
        scratch_shapes=scratch,
        compiler_params=pltpu.CompilerParams(vmem_limit_bytes=LIMIT),
        cost_estimate=pl.CostEstimate(flops=flops, bytes_accessed=1 << 20, transcendentals=0),
    )(*args)


def local(image, first_kernel, first_bias, middle_kernel, middle_bias, last_kernel, last_bias):
    slices, rows, cols = image.shape
    channels, outputs = first_kernel.shape[2], last_kernel.shape[2]
    sizes = Sizes(slices, rows, cols, channels, outputs, lax.axis_size("slab"), lax.axis_size("row"))
    t = image.transpose(0, 2, 1)
    even, odd = swap_rows(t, 0), swap_rows(t, 1)
    parameters = (
        first_kernel.reshape(3, 3, channels),
        first_bias.reshape(1, channels),
        middle_kernel,
        middle_bias.reshape(1, channels),
        last_kernel,
        last_bias.reshape(1, outputs),
    )
    own, *weights = call(
        functools.partial(prepare_kernel, sizes),
        "prepare",
        [(t.shape, BF16), *sizes.weight_shapes()],
        [pltpu.with_memory_space_constraint(p, pltpu.HBM) for p in (t, *parameters)],
        [pltpu.VMEM(p.shape, p.dtype) for p in parameters] + [pltpu.SemaphoreType.DMA((7,))],
        flops=1 << 20,
        space=pltpu.HBM,
    )
    wide = rows + 6
    e = call(extend_kernel, "extend", ((slices, cols, wide), BF16), (own, even, odd))
    swapped = [swap_slabs(e, turn_of) for turn_of in (2, 1, 0)]
    lanes = max(kind[2][1] for kind in sizes.kinds) * channels
    xy_hidden = pltpu.VMEM(((sizes.span + SUB) * SUB, LANES), F32)
    xy = call(
        functools.partial(xy_kernel, sizes),
        "xy",
        ((outputs, slices, cols, rows), F32),
        (e, *weights[YZ:]),
        [xy_hidden] * pl.cdiv(lanes, LANES),
        flops=1 << 28,
    )
    flows = call(
        functools.partial(yz_kernel, sizes),
        "yz",
        ((outputs + 1, slices, cols, rows), F32),
        (e, *swapped, xy, *weights[:YZ], weights[-1]),
        [pltpu.VMEM((sizes.padded * SUB, LANES), F32)],
        flops=1 << 28,
    )
    return flows.transpose(0, 1, 3, 2)


def solution(mesh):
    placed = (P("slab", "row", None), P(), P(), P(), P(), P(), P())
    return jax.shard_map(
        local, mesh=mesh, in_specs=placed, out_specs=P(None, "slab", "row", None), check_vma=False
    )
```

```python
import functools

import jax
import jax.numpy as jnp
from jax import lax
from jax.experimental import pallas as pl
from jax.experimental.pallas import tpu as pltpu
from jax.sharding import PartitionSpec as P

SUB = 8
LANES = 128
NEVER = -3.0e38
LIMIT = 12 << 20
F32 = jnp.float32
BF16 = jnp.bfloat16


def matching(count, parity):
    partner = {}
    for left in range(parity, count - 1, 2):
        partner[left] = left + 1
        partner[left + 1] = left
    return partner


def swap_rows(values, parity):
    count = lax.axis_size("row")
    partner = matching(count, parity)
    ends = [i for i in range(count) if i not in partner]
    for here, there in zip(ends, reversed(ends)):
        partner[here] = there
    return lax.ppermute(values, "row", sorted(partner.items()))


EARLY = 2


def slab_rounds(slabs, row):
    borders = list(range(slabs - 1))
    if row < EARLY:
        return [borders[:1] + borders[3::2], borders[1:2] + borders[4::2], borders[2:3]]
    return [borders[1::2], borders[::2], []]


def swap_slabs(values, turn_of):
    slabs, rows = lax.axis_size("slab"), lax.axis_size("row")
    across = matching(rows, 0)
    pairs = []
    for r in range(rows):
        partner = {}
        for border in slab_rounds(slabs, r)[turn_of]:
            partner[border], partner[border + 1] = border + 1, border
        for s in range(slabs):
            there = (partner[s], r) if s in partner else (s, across.get(r, r))
            pairs.append((s * rows + r, there[0] * rows + there[1]))
    return lax.ppermute(values, ("slab", "row"), sorted(pairs))


def before_and_after(even, odd, axis):
    here, count = lax.axis_index(axis), lax.axis_size(axis)
    low = here % 2 == 0
    before = jnp.where(low, odd, even)
    after = jnp.where(low, even, odd)
    before = jnp.where(here > 0, before, jnp.zeros_like(before))
    after = jnp.where(here < count - 1, after, jnp.zeros_like(after))
    return before, after


def tile_lanes(row, count):
    return jnp.concatenate([row] * count, axis=1)


def iota(shape, dim):
    return lax.broadcasted_iota(jnp.int32, shape, dim)


def nn(left, right):
    return lax.dot_general(left, right, (((1,), (0,)), ((), ())), preferred_element_type=F32)


def nt(left, right):
    return lax.dot_general(left, right, (((1,), (1,)), ((), ())), preferred_element_type=F32)


def keep_hidden(scratch, values):
    for i in range(0, values.shape[1], LANES):
        piece = values[:, i : i + LANES]
        scratch[i // LANES][: piece.shape[0], : piece.shape[1]] = piece


def gather_hidden(scratch, runs, lanes):
    columns = []
    for i in range(0, lanes, LANES):
        parts = [scratch[i // LANES][pl.ds(start, count, stride=SUB), :] for start, count in runs]
        columns.append(jnp.concatenate(parts, axis=0).astype(BF16)[:, : lanes - i])
    return jnp.concatenate(columns, axis=1)


def last_layer(w3, hidden):
    every = nt(w3[...], hidden)
    count, lanes = every.shape[0] // 3, every.shape[1] - SUB
    return sum(every[i * count : (i + 1) * count, i : i + lanes] for i in range(3))


class Sizes:
    def __init__(self, slices, rows, cols, channels, outputs, slabs, parts):
        self.slices, self.rows, self.cols = slices, rows, cols
        self.channels, self.outputs = channels, outputs
        self.slabs, self.parts = slabs, parts
        assert slices >= 3 and SUB % slices == 0
        self.halves = SUB // slices
        assert rows % self.halves == 0 and cols % SUB == 0
        self.span = rows // self.halves
        self.padded = -(-outputs * slices // SUB) * SUB
        self.slot = rows + SUB
        self.chunks = []
        self.kinds = []
        for start in range(0, cols, SUB):
            ranges = []
            for reach in (3, 2, 1, 0):
                low = max(0, start - reach)
                ranges.append((low - start, min(cols, start + SUB + reach) - low))
            kind = tuple(ranges)
            if kind not in self.kinds:
                self.kinds.append(kind)
            self.chunks.append((start, self.kinds.index(kind)))

    def weight_shapes(self):
        c, z = self.channels, self.slices
        shapes = [
            ((3 * (z + 6) * SUB, (z + 4) * c), BF16),
            ((3, (z + 4) * c, (z + 2) * c), BF16),
            ((3 * self.padded, (z + 2) * c), BF16),
            ((1, (z + 4) * c), F32),
            ((1, (z + 2) * c), F32),
        ]
        for image, one, two, _ in self.kinds:
            shapes += [
                ((3 * z * image[1], one[1] * c), BF16),
                ((3, one[1] * c, two[1] * c), BF16),
                ((3 * self.outputs * SUB, two[1] * c), BF16),
                ((1, one[1] * c), F32),
                ((1, two[1] * c), F32),
            ]
        return shapes + [((self.outputs, SUB, self.rows), F32)]


def banded(blocks, out_count, in_count, offset):
    zero = jnp.zeros_like(blocks[0])
    lines = []
    for inner in range(in_count):
        line = []
        for out in range(out_count):
            tap = inner - out + offset
            line.append(blocks[tap] if 0 <= tap < 3 else zero)
        lines.append(jnp.concatenate(line, axis=1))
    return jnp.concatenate(lines, axis=0)


def spread(tap_of, group_of, shape, lines):
    total = jnp.zeros(shape, F32)
    for (group, tap), line in lines.items():
        total = jnp.where((tap_of == tap) & (group_of == group), line, total)
    return total.astype(BF16)


def prepare_kernel(sizes, *refs):
    count = 7
    arguments, outs, held, sems = refs[:count], refs[count:-count], refs[-count:-1], refs[-1]
    t_out, *outs = outs
    copies = [
        pltpu.make_async_copy(here, there, sems.at[i])
        for i, (here, there) in enumerate(zip(arguments, (t_out, *held)))
    ]
    for copy in copies:
        copy.start()
    for copy in copies:
        copy.wait()
    c, z, n_out = sizes.channels, sizes.slices, sizes.outputs
    k1_ref, b1_ref, k2_ref, b2_ref, k3_ref, b3_ref = held
    k1 = k1_ref[...].astype(F32)
    k3 = k3_ref[...].astype(F32)
    b1, b2 = b1_ref[...], b2_ref[...]

    k2 = [[k2_ref[a, b].astype(F32).T.astype(BF16) for b in range(3)] for a in range(3)]

    def first(ref, tap_of, tap_index):
        rows, lanes = ref.shape[0] // 3, ref.shape[1]
        for shift in range(3):
            lines = {(0, t): tile_lanes(k1[tap_index(shift, t)][None, :], lanes // c) for t in range(3)}
            ref[shift * rows : (shift + 1) * rows, :] = spread(tap_of, 0, (rows, lanes), lines)

    def last(shape, group_of, tap_of, tap_index, shift):
        lines = {
            (g, t): tile_lanes(k3[tap_index(shift, t)][g][None, :], shape[1] // c)
            for g in range(n_out)
            for t in range(3)
        }
        return spread(tap_of, group_of, shape, lines)

    def along_z(shift, t):
        return t, shift

    def along_x(shift, t):
        return shift, t

    w1, w2, w3, c1, c2 = outs[:5]
    shape = (w1.shape[0] // 3, w1.shape[1])
    first(w1, iota(shape, 0) // SUB - iota(shape, 1) // c, along_z)
    shape = (w3.shape[0] // 3, w3.shape[1])
    row = iota(shape, 0)
    for b in range(3):
        w2[b] = banded([k2[a][b] for a in range(3)], z + 2, z + 4, 0)
        w3[b * shape[0] : (b + 1) * shape[0], :] = last(
            shape, row // z, iota(shape, 1) // c - row % z, along_z, b
        )
    base = lax.axis_index("slab") * z
    for ref, bias, reach in ((c1, b1, 2), (c2, b2, 1)):
        where = base + iota(ref.shape, 1) // c - reach
        inside = (where >= 0) & (where < sizes.slabs * z)
        ref[...] = jnp.where(inside, tile_lanes(bias, ref.shape[1] // c), NEVER)

    for index, (image, one, two, out) in enumerate(sizes.kinds):
        w1, w2, w3, c1, c2 = outs[5 + 5 * index : 10 + 5 * index]
        shape = (w1.shape[0] // 3, w1.shape[1])
        first(w1, iota(shape, 0) % image[1] + image[0] - iota(shape, 1) // c - one[0] + 1, along_x)
        shape = (w3.shape[0] // 3, w3.shape[1])
        row = iota(shape, 0)
        tap = iota(shape, 1) // c + two[0] - row % SUB - out[0] + 1
        for a in range(3):
            w2[a] = banded([k2[a][b] for b in range(3)], two[1], one[1], one[0] - two[0] + 1)
            w3[a * shape[0] : (a + 1) * shape[0], :] = last(shape, row // SUB, tap, along_x, a)
        c1[...] = tile_lanes(b1, one[1])
        c2[...] = tile_lanes(b2, two[1])
    for g in range(n_out):
        outs[-1][g] = jnp.broadcast_to(b3_ref[0:1, g : g + 1], (SUB, sizes.rows))


def extend_kernel(own_ref, even_ref, odd_ref, out_ref):
    rows = own_ref.shape[2]
    before, after = before_and_after(even_ref[...], odd_ref[...], "row")
    out_ref[...] = jnp.concatenate([before[:, :, rows - 3 :], own_ref[...], after[:, :, :3]], axis=2)


def zero_groups(values, count, low, high):
    edge = count * SUB
    top, middle, bottom = values[:edge], values[edge:-edge], values[-edge:]
    if low.ndim:
        low, high = low[:edge], high[:edge]
    return jnp.concatenate([jnp.where(low, 0.0, top), middle, jnp.where(high, 0.0, bottom)], axis=0)


def taps(values, count):
    low, high = values.astype(BF16), values[SUB:].astype(BF16)
    return [low[:count], high[:count], low[2 * SUB : 2 * SUB + count]]


def pick(select, e):
    count = select.shape[1]
    return nt(select, jnp.concatenate([e[:, shift : shift + count] for shift in range(3)], axis=0))


def hidden_layers(picked, w1, w2, c1, c2, low, high):
    n2 = picked.shape[0] - 2 * SUB
    one = nn(picked.astype(BF16), w1[...])
    one = zero_groups(jnp.maximum(one + c1[...], 0.0), 2, low, high)
    two = sum(nn(tap, w2[i]) for i, tap in enumerate(taps(one, n2)))
    return zero_groups(jnp.maximum(two + c2[...], 0.0), 1, low, high)


def xy_kernel(sizes, e_ref, *refs):
    count = sum(1 for _ in sizes.kinds) * 5
    weights, (b3, out_ref, *hidden) = refs[:count], refs[count:]
    z, span = sizes.slices, sizes.span
    wide = sizes.rows + 6
    row = lax.axis_index("row")
    half = iota((2 * SUB, 1), 0) % SUB // z
    low = (row == 0) & (half == 0)
    high = (row == sizes.parts - 1) & (half == sizes.halves - 1)
    shape = ((span + 4) * SUB, sizes.rows + 4)
    wanted = iota(shape, 0) // SUB + iota(shape, 0) % SUB // z * span
    select = jnp.where(iota(shape, 1) == wanted, 1.0, 0.0).astype(BF16)
    for start, index in sizes.chunks:
        image = sizes.kinds[index][0]
        w1, w2, w3, c1, c2 = weights[5 * index : 5 * index + 5]
        low_col = start + image[0]
        e = e_ref[:, low_col : low_col + image[1], :].reshape(z * image[1], wide)
        picked = pick(select, e)
        same = iota(picked.shape, 1) // image[1] % z == iota(picked.shape, 0) % z
        picked = jnp.where(same, picked, 0.0)
        second = hidden_layers(picked, w1, w2, c1, c2, low, high)
        keep_hidden(hidden, second)
        runs = [
            (h * z + s, span if h < sizes.halves - 1 else span + SUB)
            for s in range(z)
            for h in range(sizes.halves)
        ]
        total = last_layer(w3, gather_hidden(hidden, runs, second.shape[1]))
        for g in range(sizes.outputs):
            for s in range(z):
                piece = total[g * SUB : (g + 1) * SUB, s * sizes.slot : s * sizes.slot + sizes.rows]
                out_ref[g, s, start : start + SUB, :] = piece + b3[g]


def yz_kernel(sizes, e_ref, round_2, round_1, round_0, xy_ref, w1, w2, w3, c1, c2, b3, out_ref, turned, *hidden):
    z = sizes.slices
    wide = sizes.rows + 6
    row = lax.axis_index("row")
    low, high = row == 0, row == sizes.parts - 1
    slab = lax.axis_index("slab")
    early = lax.axis_index("row") < EARLY
    swapped = [ref[...] for ref in (round_0, round_1, round_2)]
    even = jnp.where(early & (slab < 2), swapped[0], swapped[1])
    even = jnp.where(early & (slab >= 2) & (slab < 4), swapped[2], even)
    odd = jnp.where(early & (slab >= 1) & (slab < 3), swapped[1], swapped[0])
    before, after = before_and_after(even, odd, "slab")
    block = jnp.concatenate([before[z - 3 :], e_ref[...], after[:3]], axis=0)
    shape = ((sizes.rows + 4) * SUB, sizes.rows + 4)
    select = jnp.where(iota(shape, 1) == iota(shape, 0) // SUB, 1.0, 0.0).astype(BF16)
    for start in range(0, sizes.cols, SUB):
        e = block[:, start : start + SUB, :].reshape((z + 6) * SUB, wide)
        flat = e.astype(F32).T
        count = sizes.rows + 4
        flat = jnp.concatenate([flat[shift : shift + count] for shift in range(3)], axis=1)
        picked = jnp.broadcast_to(flat[:, None, :], (count, SUB, flat.shape[1])).reshape(count * SUB, flat.shape[1])
        same = iota(picked.shape, 1) % SUB == iota(picked.shape, 0) % SUB
        picked = jnp.where(same, picked, 0.0)
        two = hidden_layers(picked, w1, w2, c1, c2, low, high)
        keep_hidden(hidden, two)
        runs = [(x, sizes.slot) for x in range(SUB)]
        total = last_layer(w3, gather_hidden(hidden, runs, two.shape[1]))
        rest = jnp.zeros((total.shape[0], LANES - sizes.rows), F32)
        for x in range(SUB):
            piece = total[:, x * sizes.slot : x * sizes.slot + sizes.rows]
            turned[pl.ds(x, total.shape[0], stride=SUB), :] = jnp.concatenate([piece, rest], axis=1)
        for s in range(z):
            yz = [turned[(g * z + s) * SUB : (g * z + s + 1) * SUB, : sizes.rows] + b3[g] for g in range(3)]
            here = slice(start, start + SUB)
            out_ref[0, s, here, :] = yz[0]
            out_ref[1, s, here, :] = 0.5 * (xy_ref[0, s, here, :] + yz[1])
            out_ref[2, s, here, :] = xy_ref[1, s, here, :]
            out_ref[3, s, here, :] = 0.5 * (xy_ref[2, s, here, :] + yz[2])


def call(kernel, name, outs, args, scratch=(), flops=0, space=pltpu.VMEM):
    single = not isinstance(outs, list)
    shapes = [jax.ShapeDtypeStruct(shape, kind) for shape, kind in ([outs] if single else outs)]
    return pl.pallas_call(
        kernel,
        name=name,
        out_shape=shapes[0] if single else shapes,
        in_specs=[pl.BlockSpec(memory_space=space)] * len(args),
        scratch_shapes=scratch,
        compiler_params=pltpu.CompilerParams(vmem_limit_bytes=LIMIT),
        cost_estimate=pl.CostEstimate(flops=flops, bytes_accessed=1 << 20, transcendentals=0),
    )(*args)


def local(image, first_kernel, first_bias, middle_kernel, middle_bias, last_kernel, last_bias):
    slices, rows, cols = image.shape
    channels, outputs = first_kernel.shape[2], last_kernel.shape[2]
    sizes = Sizes(slices, rows, cols, channels, outputs, lax.axis_size("slab"), lax.axis_size("row"))
    t = image.transpose(0, 2, 1)
    even, odd = swap_rows(t, 0), swap_rows(t, 1)
    parameters = (
        first_kernel.reshape(3, 3, channels),
        first_bias.reshape(1, channels),
        middle_kernel,
        middle_bias.reshape(1, channels),
        last_kernel,
        last_bias.reshape(1, outputs),
    )
    own, *weights = call(
        functools.partial(prepare_kernel, sizes),
        "prepare",
        [(t.shape, BF16), *sizes.weight_shapes()],
        [pltpu.with_memory_space_constraint(p, pltpu.HBM) for p in (t, *parameters)],
        [pltpu.VMEM(p.shape, p.dtype) for p in parameters] + [pltpu.SemaphoreType.DMA((7,))],
        flops=1 << 20,
        space=pltpu.HBM,
    )
    wide = rows + 6
    e = call(extend_kernel, "extend", ((slices, cols, wide), BF16), (own, even, odd))
    swapped = [swap_slabs(e, turn_of) for turn_of in (2, 1, 0)]
    lanes = max(kind[2][1] for kind in sizes.kinds) * channels
    xy_hidden = pltpu.VMEM(((sizes.span + SUB) * SUB, LANES), F32)
    yz_hidden = pltpu.VMEM((sizes.slot * SUB, LANES), F32)
    xy = call(
        functools.partial(xy_kernel, sizes),
        "xy",
        ((outputs, slices, cols, rows), F32),
        (e, *weights[5:]),
        [xy_hidden] * pl.cdiv(lanes, LANES),
        flops=1 << 28,
    )
    flows = call(
        functools.partial(yz_kernel, sizes),
        "yz",
        ((outputs + 1, slices, cols, rows), F32),
        (e, *swapped, xy, *weights[:5], weights[-1]),
        [pltpu.VMEM((sizes.padded * SUB, LANES), F32)]
        + [yz_hidden] * pl.cdiv((slices + 2) * channels, LANES),
        flops=1 << 28,
    )
    return flows.transpose(0, 1, 3, 2)


def solution(mesh):
    placed = (P("slab", "row", None), P(), P(), P(), P(), P(), P())
    return jax.shard_map(
        local, mesh=mesh, in_specs=placed, out_specs=P(None, "slab", "row", None), check_vma=False
    )
```

```python
import functools

import jax
import jax.numpy as jnp
from jax import lax
from jax.experimental import pallas as pl
from jax.experimental.pallas import tpu as pltpu
from jax.sharding import PartitionSpec as P

SUB = 8
LANES = 128
NEVER = -3.0e38
LIMIT = 12 << 20
F32 = jnp.float32
BF16 = jnp.bfloat16


def matching(count, parity):
    partner = {}
    for left in range(parity, count - 1, 2):
        partner[left] = left + 1
        partner[left + 1] = left
    return partner


def swap_rows(values, parity):
    count = lax.axis_size("row")
    partner = matching(count, parity)
    ends = [i for i in range(count) if i not in partner]
    for here, there in zip(ends, reversed(ends)):
        partner[here] = there
    return lax.ppermute(values, "row", sorted(partner.items()))


EARLY = 2


def slab_rounds(slabs, row):
    borders = list(range(slabs - 1))
    if row < EARLY:
        return [borders[:1] + borders[3::2], borders[1:2] + borders[4::2], borders[2:3]]
    return [borders[1::2], borders[::2], []]


def swap_slabs(values, turn_of):
    slabs, rows = lax.axis_size("slab"), lax.axis_size("row")
    across = matching(rows, 0)
    pairs = []
    for r in range(rows):
        partner = {}
        for border in slab_rounds(slabs, r)[turn_of]:
            partner[border], partner[border + 1] = border + 1, border
        for s in range(slabs):
            there = (partner[s], r) if s in partner else (s, across.get(r, r))
            pairs.append((s * rows + r, there[0] * rows + there[1]))
    return lax.ppermute(values, ("slab", "row"), sorted(pairs))


def before_and_after(even, odd, axis):
    here, count = lax.axis_index(axis), lax.axis_size(axis)
    low = here % 2 == 0
    before = jnp.where(low, odd, even)
    after = jnp.where(low, even, odd)
    before = jnp.where(here > 0, before, jnp.zeros_like(before))
    after = jnp.where(here < count - 1, after, jnp.zeros_like(after))
    return before, after


def tile_lanes(row, count):
    return jnp.concatenate([row] * count, axis=1)


def iota(shape, dim):
    return lax.broadcasted_iota(jnp.int32, shape, dim)


def nn(left, right):
    return lax.dot_general(left, right, (((1,), (0,)), ((), ())), preferred_element_type=F32)


def nt(left, right):
    return lax.dot_general(left, right, (((1,), (1,)), ((), ())), preferred_element_type=F32)


def keep_hidden(scratch, values):
    for i in range(0, values.shape[1], LANES):
        piece = values[:, i : i + LANES]
        scratch[i // LANES][: piece.shape[0], : piece.shape[1]] = piece


def gather_hidden(scratch, runs, lanes):
    columns = []
    for i in range(0, lanes, LANES):
        parts = [scratch[i // LANES][pl.ds(start, count, stride=SUB), :] for start, count in runs]
        columns.append(jnp.concatenate(parts, axis=0).astype(BF16)[:, : lanes - i])
    return jnp.concatenate(columns, axis=1)


def last_layer(w3, hidden):
    every = nt(w3[...], hidden)
    count, lanes = every.shape[0] // 3, every.shape[1] - SUB
    return sum(every[i * count : (i + 1) * count, i : i + lanes] for i in range(3))


class Sizes:
    def __init__(self, slices, rows, cols, channels, outputs, slabs, parts):
        self.slices, self.rows, self.cols = slices, rows, cols
        self.channels, self.outputs = channels, outputs
        self.slabs, self.parts = slabs, parts
        assert slices >= 3 and SUB % slices == 0
        self.halves = SUB // slices
        assert rows % self.halves == 0 and cols % SUB == 0
        self.span = rows // self.halves
        self.padded = -(-outputs * slices // SUB) * SUB
        self.slot = rows + SUB
        self.chunks = []
        self.kinds = []
        for start in range(0, cols, SUB):
            ranges = []
            for reach in (3, 2, 1, 0):
                low = max(0, start - reach)
                ranges.append((low - start, min(cols, start + SUB + reach) - low))
            kind = tuple(ranges)
            if kind not in self.kinds:
                self.kinds.append(kind)
            self.chunks.append((start, self.kinds.index(kind)))

    def weight_shapes(self):
        c, z = self.channels, self.slices
        shapes = [
            ((3 * (z + 6) * SUB, (z + 4) * c), BF16),
            ((3, (z + 4) * c, (z + 2) * c), BF16),
            ((3 * self.padded, (z + 2) * c), BF16),
            ((1, (z + 4) * c), F32),
            ((1, (z + 2) * c), F32),
        ]
        for image, one, two, _ in self.kinds:
            shapes += [
                ((3 * z * image[1], one[1] * c), BF16),
                ((3, one[1] * c, two[1] * c), BF16),
                ((3 * self.outputs * SUB, two[1] * c), BF16),
                ((1, one[1] * c), F32),
                ((1, two[1] * c), F32),
            ]
        return shapes + [((self.outputs, SUB, self.rows), F32)]


def banded(blocks, out_count, in_count, offset):
    zero = jnp.zeros_like(blocks[0])
    lines = []
    for inner in range(in_count):
        line = []
        for out in range(out_count):
            tap = inner - out + offset
            line.append(blocks[tap] if 0 <= tap < 3 else zero)
        lines.append(jnp.concatenate(line, axis=1))
    return jnp.concatenate(lines, axis=0)


def spread(tap_of, group_of, shape, lines):
    total = jnp.zeros(shape, F32)
    for (group, tap), line in lines.items():
        total = jnp.where((tap_of == tap) & (group_of == group), line, total)
    return total.astype(BF16)


def prepare_kernel(sizes, *refs):
    count = 7
    arguments, outs, held, sems = refs[:count], refs[count:-count], refs[-count:-1], refs[-1]
    t_out, *outs = outs
    copies = [
        pltpu.make_async_copy(here, there, sems.at[i])
        for i, (here, there) in enumerate(zip(arguments, (t_out, *held)))
    ]
    for copy in copies:
        copy.start()
    for copy in copies:
        copy.wait()
    c, z, n_out = sizes.channels, sizes.slices, sizes.outputs
    k1_ref, b1_ref, k2_ref, b2_ref, k3_ref, b3_ref = held
    k1 = k1_ref[...].astype(F32)
    k3 = k3_ref[...].astype(F32)
    b1, b2 = b1_ref[...], b2_ref[...]

    k2 = [[k2_ref[a, b].astype(F32).T.astype(BF16) for b in range(3)] for a in range(3)]

    def first(ref, tap_of, tap_index):
        rows, lanes = ref.shape[0] // 3, ref.shape[1]
        for shift in range(3):
            lines = {(0, t): tile_lanes(k1[tap_index(shift, t)][None, :], lanes // c) for t in range(3)}
            ref[shift * rows : (shift + 1) * rows, :] = spread(tap_of, 0, (rows, lanes), lines)

    def last(shape, group_of, tap_of, tap_index, shift):
        lines = {
            (g, t): tile_lanes(k3[tap_index(shift, t)][g][None, :], shape[1] // c)
            for g in range(n_out)
            for t in range(3)
        }
        return spread(tap_of, group_of, shape, lines)

    def along_z(shift, t):
        return t, shift

    def along_x(shift, t):
        return shift, t

    w1, w2, w3, c1, c2 = outs[:5]
    shape = (w1.shape[0] // 3, w1.shape[1])
    first(w1, iota(shape, 0) // SUB - iota(shape, 1) // c, along_z)
    shape = (w3.shape[0] // 3, w3.shape[1])
    row = iota(shape, 0)
    for b in range(3):
        w2[b] = banded([k2[a][b] for a in range(3)], z + 2, z + 4, 0)
        w3[b * shape[0] : (b + 1) * shape[0], :] = last(
            shape, row // z, iota(shape, 1) // c - row % z, along_z, b
        )
    base = lax.axis_index("slab") * z
    for ref, bias, reach in ((c1, b1, 2), (c2, b2, 1)):
        where = base + iota(ref.shape, 1) // c - reach
        inside = (where >= 0) & (where < sizes.slabs * z)
        ref[...] = jnp.where(inside, tile_lanes(bias, ref.shape[1] // c), NEVER)

    for index, (image, one, two, out) in enumerate(sizes.kinds):
        w1, w2, w3, c1, c2 = outs[5 + 5 * index : 10 + 5 * index]
        shape = (w1.shape[0] // 3, w1.shape[1])
        first(w1, iota(shape, 0) % image[1] + image[0] - iota(shape, 1) // c - one[0] + 1, along_x)
        shape = (w3.shape[0] // 3, w3.shape[1])
        row = iota(shape, 0)
        tap = iota(shape, 1) // c + two[0] - row % SUB - out[0] + 1
        for a in range(3):
            w2[a] = banded([k2[a][b] for b in range(3)], two[1], one[1], one[0] - two[0] + 1)
            w3[a * shape[0] : (a + 1) * shape[0], :] = last(shape, row // SUB, tap, along_x, a)
        c1[...] = tile_lanes(b1, one[1])
        c2[...] = tile_lanes(b2, two[1])
    for g in range(n_out):
        outs[-1][g] = jnp.broadcast_to(b3_ref[0:1, g : g + 1], (SUB, sizes.rows))


def extend_kernel(own_ref, even_ref, odd_ref, out_ref):
    rows = own_ref.shape[2]
    before, after = before_and_after(even_ref[...], odd_ref[...], "row")
    out_ref[...] = jnp.concatenate([before[:, :, rows - 3 :], own_ref[...], after[:, :, :3]], axis=2)


def zero_groups(values, count, low, high):
    edge = count * SUB
    top, middle, bottom = values[:edge], values[edge:-edge], values[-edge:]
    if low.ndim:
        low, high = low[:edge], high[:edge]
    return jnp.concatenate([jnp.where(low, 0.0, top), middle, jnp.where(high, 0.0, bottom)], axis=0)


def taps(values, count):
    low, high = values.astype(BF16), values[SUB:].astype(BF16)
    return [low[:count], high[:count], low[2 * SUB : 2 * SUB + count]]


def pick(select, e):
    count = select.shape[1]
    return nt(select, jnp.concatenate([e[:, shift : shift + count] for shift in range(3)], axis=0))


def hidden_layers(picked, w1, w2, c1, c2, low, high):
    n2 = picked.shape[0] - 2 * SUB
    one = nn(picked.astype(BF16), w1[...])
    one = zero_groups(jnp.maximum(one + c1[...], 0.0), 2, low, high)
    two = sum(nn(tap, w2[i]) for i, tap in enumerate(taps(one, n2)))
    return zero_groups(jnp.maximum(two + c2[...], 0.0), 1, low, high)


def xy_kernel(sizes, e_ref, *refs):
    count = sum(1 for _ in sizes.kinds) * 5
    weights, (b3, out_ref, *hidden) = refs[:count], refs[count:]
    z, span = sizes.slices, sizes.span
    wide = sizes.rows + 6
    row = lax.axis_index("row")
    half = iota((2 * SUB, 1), 0) % SUB // z
    low = (row == 0) & (half == 0)
    high = (row == sizes.parts - 1) & (half == sizes.halves - 1)
    shape = ((span + 4) * SUB, sizes.rows + 4)
    wanted = iota(shape, 0) // SUB + iota(shape, 0) % SUB // z * span
    select = jnp.where(iota(shape, 1) == wanted, 1.0, 0.0).astype(BF16)
    for start, index in sizes.chunks:
        image = sizes.kinds[index][0]
        w1, w2, w3, c1, c2 = weights[5 * index : 5 * index + 5]
        low_col = start + image[0]
        e = e_ref[:, low_col : low_col + image[1], :].reshape(z * image[1], wide)
        picked = pick(select, e)
        same = iota(picked.shape, 1) // image[1] % z == iota(picked.shape, 0) % z
        picked = jnp.where(same, picked, 0.0)
        second = hidden_layers(picked, w1, w2, c1, c2, low, high)
        keep_hidden(hidden, second)
        runs = [
            (h * z + s, span if h < sizes.halves - 1 else span + SUB)
            for s in range(z)
            for h in range(sizes.halves)
        ]
        total = last_layer(w3, gather_hidden(hidden, runs, second.shape[1]))
        here = slice(start, start + SUB)
        for s in range(z):
            xy = [
                total[g * SUB : (g + 1) * SUB, s * sizes.slot : s * sizes.slot + sizes.rows] + b3[g] for g in range(3)
            ]
            out_ref[0, s, here, :] = b3[0]
            out_ref[1, s, here, :] = 0.5 * (xy[0] + b3[1])
            out_ref[2, s, here, :] = xy[1]
            out_ref[3, s, here, :] = 0.5 * (xy[2] + b3[2])


def yz_kernel(sizes, e_ref, round_2, round_1, round_0, base_ref, w1, w2, w3, c1, c2, out_ref, turned, *hidden):
    z = sizes.slices
    wide = sizes.rows + 6
    row = lax.axis_index("row")
    low, high = row == 0, row == sizes.parts - 1
    slab = lax.axis_index("slab")
    early = lax.axis_index("row") < EARLY
    swapped = [ref[...] for ref in (round_0, round_1, round_2)]
    even = jnp.where(early & (slab < 2), swapped[0], swapped[1])
    even = jnp.where(early & (slab >= 2) & (slab < 4), swapped[2], even)
    odd = jnp.where(early & (slab >= 1) & (slab < 3), swapped[1], swapped[0])
    before, after = before_and_after(even, odd, "slab")
    block = jnp.concatenate([before[z - 3 :], e_ref[...], after[:3]], axis=0)
    shape = ((sizes.rows + 4) * SUB, sizes.rows + 4)
    select = jnp.where(iota(shape, 1) == iota(shape, 0) // SUB, 1.0, 0.0).astype(BF16)
    for start in range(0, sizes.cols, SUB):
        e = block[:, start : start + SUB, :].reshape((z + 6) * SUB, wide)
        flat = e.astype(F32).T
        count = sizes.rows + 4
        flat = jnp.concatenate([flat[shift : shift + count] for shift in range(3)], axis=1)
        picked = jnp.broadcast_to(flat[:, None, :], (count, SUB, flat.shape[1])).reshape(count * SUB, flat.shape[1])
        same = iota(picked.shape, 1) % SUB == iota(picked.shape, 0) % SUB
        picked = jnp.where(same, picked, 0.0)
        two = hidden_layers(picked, w1, w2, c1, c2, low, high)
        keep_hidden(hidden, two)
        runs = [(x, sizes.slot) for x in range(SUB)]
        total = last_layer(w3, gather_hidden(hidden, runs, two.shape[1]))
        rest = jnp.zeros((total.shape[0], LANES - sizes.rows), F32)
        for x in range(SUB):
            piece = total[:, x * sizes.slot : x * sizes.slot + sizes.rows]
            turned[pl.ds(x, total.shape[0], stride=SUB), :] = jnp.concatenate([piece, rest], axis=1)
        here = slice(start, start + SUB)
        for s in range(z):
            yz = [turned[(g * z + s) * SUB : (g * z + s + 1) * SUB, : sizes.rows] for g in range(3)]
            out_ref[0, s, here, :] = base_ref[0, s, here, :] + yz[0]
            out_ref[1, s, here, :] = base_ref[1, s, here, :] + 0.5 * yz[1]
            out_ref[2, s, here, :] = base_ref[2, s, here, :]
            out_ref[3, s, here, :] = base_ref[3, s, here, :] + 0.5 * yz[2]


def call(kernel, name, outs, args, scratch=(), flops=0, space=pltpu.VMEM):
    single = not isinstance(outs, list)
    shapes = [jax.ShapeDtypeStruct(shape, kind) for shape, kind in ([outs] if single else outs)]
    return pl.pallas_call(
        kernel,
        name=name,
        out_shape=shapes[0] if single else shapes,
        in_specs=[pl.BlockSpec(memory_space=space)] * len(args),
        scratch_shapes=scratch,
        compiler_params=pltpu.CompilerParams(vmem_limit_bytes=LIMIT),
        cost_estimate=pl.CostEstimate(flops=flops, bytes_accessed=1 << 20, transcendentals=0),
    )(*args)


def local(image, first_kernel, first_bias, middle_kernel, middle_bias, last_kernel, last_bias):
    slices, rows, cols = image.shape
    channels, outputs = first_kernel.shape[2], last_kernel.shape[2]
    sizes = Sizes(slices, rows, cols, channels, outputs, lax.axis_size("slab"), lax.axis_size("row"))
    t = image.transpose(0, 2, 1)
    even, odd = swap_rows(t, 0), swap_rows(t, 1)
    parameters = (
        first_kernel.reshape(3, 3, channels),
        first_bias.reshape(1, channels),
        middle_kernel,
        middle_bias.reshape(1, channels),
        last_kernel,
        last_bias.reshape(1, outputs),
    )
    own, *weights = call(
        functools.partial(prepare_kernel, sizes),
        "prepare",
        [(t.shape, BF16), *sizes.weight_shapes()],
        [pltpu.with_memory_space_constraint(p, pltpu.HBM) for p in (t, *parameters)],
        [pltpu.VMEM(p.shape, p.dtype) for p in parameters] + [pltpu.SemaphoreType.DMA((7,))],
        flops=1 << 20,
        space=pltpu.HBM,
    )
    wide = rows + 6
    e = call(extend_kernel, "extend", ((slices, cols, wide), BF16), (own, even, odd))
    swapped = [swap_slabs(e, turn_of) for turn_of in (2, 1, 0)]
    lanes = max(kind[2][1] for kind in sizes.kinds) * channels
    xy_hidden = pltpu.VMEM(((sizes.span + SUB) * SUB, LANES), F32)
    yz_hidden = pltpu.VMEM((sizes.slot * SUB, LANES), F32)
    base = call(
        functools.partial(xy_kernel, sizes),
        "xy",
        ((outputs + 1, slices, cols, rows), F32),
        (e, *weights[5:]),
        [xy_hidden] * pl.cdiv(lanes, LANES),
        flops=1 << 28,
    )
    flows = call(
        functools.partial(yz_kernel, sizes),
        "yz",
        ((outputs + 1, slices, cols, rows), F32),
        (e, *swapped, base, *weights[:5]),
        [pltpu.VMEM((sizes.padded * SUB, LANES), F32)]
        + [yz_hidden] * pl.cdiv((slices + 2) * channels, LANES),
        flops=1 << 28,
    )
    return flows.transpose(0, 1, 3, 2)


def solution(mesh):
    placed = (P("slab", "row", None), P(), P(), P(), P(), P(), P())
    return jax.shard_map(
        local, mesh=mesh, in_specs=placed, out_specs=P(None, "slab", "row", None), check_vma=False
    )
```

```python
import functools

import jax
import jax.numpy as jnp
from jax import lax
from jax.experimental import pallas as pl
from jax.experimental.pallas import tpu as pltpu
from jax.sharding import PartitionSpec as P

SUB = 8
LANES = 128
NEVER = -3.0e38
LIMIT = 12 << 20
F32 = jnp.float32
BF16 = jnp.bfloat16


def matching(count, parity):
    partner = {}
    for left in range(parity, count - 1, 2):
        partner[left] = left + 1
        partner[left + 1] = left
    return partner


def swap_rows(values, parity):
    count = lax.axis_size("row")
    partner = matching(count, parity)
    ends = [i for i in range(count) if i not in partner]
    for here, there in zip(ends, reversed(ends)):
        partner[here] = there
    return lax.ppermute(values, "row", sorted(partner.items()))


EARLY = 2


def slab_rounds(slabs, row):
    borders = list(range(slabs - 1))
    if row < EARLY:
        return [borders[:1] + borders[3::2], borders[1:2] + borders[4::2], borders[2:3]]
    return [borders[1::2], borders[::2], []]


def swap_slabs(values, turn_of):
    slabs, rows = lax.axis_size("slab"), lax.axis_size("row")
    across = matching(rows, 0)
    pairs = []
    for r in range(rows):
        partner = {}
        for border in slab_rounds(slabs, r)[turn_of]:
            partner[border], partner[border + 1] = border + 1, border
        for s in range(slabs):
            there = (partner[s], r) if s in partner else (s, across.get(r, r))
            pairs.append((s * rows + r, there[0] * rows + there[1]))
    return lax.ppermute(values, ("slab", "row"), sorted(pairs))


def before_and_after(even, odd, axis):
    here, count = lax.axis_index(axis), lax.axis_size(axis)
    low = here % 2 == 0
    before = jnp.where(low, odd, even)
    after = jnp.where(low, even, odd)
    before = jnp.where(here > 0, before, jnp.zeros_like(before))
    after = jnp.where(here < count - 1, after, jnp.zeros_like(after))
    return before, after


def tile_lanes(row, count):
    return jnp.concatenate([row] * count, axis=1)


def iota(shape, dim):
    return lax.broadcasted_iota(jnp.int32, shape, dim)


def nn(left, right):
    return lax.dot_general(left, right, (((1,), (0,)), ((), ())), preferred_element_type=F32)


def nt(left, right):
    return lax.dot_general(left, right, (((1,), (1,)), ((), ())), preferred_element_type=F32)


def keep_hidden(scratch, values):
    for i in range(0, values.shape[1], LANES):
        piece = values[:, i : i + LANES]
        scratch[i // LANES][: piece.shape[0], : piece.shape[1]] = piece


def gather_hidden(scratch, runs, lanes):
    columns = []
    for i in range(0, lanes, LANES):
        parts = [scratch[i // LANES][pl.ds(start, count, stride=SUB), :] for start, count in runs]
        columns.append(jnp.concatenate(parts, axis=0).astype(BF16)[:, : lanes - i])
    return jnp.concatenate(columns, axis=1)


def last_layer(w3, hidden):
    every = nt(w3[...], hidden)
    count, lanes = every.shape[0] // 3, every.shape[1] - SUB
    return sum(every[i * count : (i + 1) * count, i : i + lanes] for i in range(3))


class Sizes:
    def __init__(self, slices, rows, cols, channels, outputs, slabs, parts):
        self.slices, self.rows, self.cols = slices, rows, cols
        self.channels, self.outputs = channels, outputs
        self.slabs, self.parts = slabs, parts
        assert slices >= 3 and SUB % slices == 0
        self.halves = SUB // slices
        assert rows % self.halves == 0 and cols % SUB == 0
        self.span = rows // self.halves
        self.padded = -(-outputs * slices // SUB) * SUB
        self.slot = rows + SUB
        self.chunks = []
        self.kinds = []
        for start in range(0, cols, SUB):
            ranges = []
            for reach in (3, 2, 1, 0):
                low = max(0, start - reach)
                ranges.append((low - start, min(cols, start + SUB + reach) - low))
            kind = tuple(ranges)
            if kind not in self.kinds:
                self.kinds.append(kind)
            self.chunks.append((start, self.kinds.index(kind)))

    def weight_shapes(self):
        c, z = self.channels, self.slices
        shapes = [
            ((3 * (z + 6) * SUB, (z + 4) * c), BF16),
            ((3, (z + 4) * c, (z + 2) * c), BF16),
            ((3 * self.padded, (z + 2) * c), BF16),
            ((1, (z + 4) * c), F32),
            ((1, (z + 2) * c), F32),
        ]
        for image, one, two, _ in self.kinds:
            shapes += [
                ((3 * z * image[1], one[1] * c), BF16),
                ((3, one[1] * c, two[1] * c), BF16),
                ((3 * self.outputs * SUB, two[1] * c), BF16),
                ((1, one[1] * c), F32),
                ((1, two[1] * c), F32),
            ]
        return shapes + [((self.outputs, SUB, self.rows), F32)]


def banded(blocks, out_count, in_count, offset):
    zero = jnp.zeros_like(blocks[0])
    lines = []
    for inner in range(in_count):
        line = []
        for out in range(out_count):
            tap = inner - out + offset
            line.append(blocks[tap] if 0 <= tap < 3 else zero)
        lines.append(jnp.concatenate(line, axis=1))
    return jnp.concatenate(lines, axis=0)


def spread(tap_of, group_of, shape, lines):
    total = jnp.zeros(shape, F32)
    for (group, tap), line in lines.items():
        total = jnp.where((tap_of == tap) & (group_of == group), line, total)
    return total.astype(BF16)


def prepare_kernel(sizes, *refs):
    count = 7
    arguments, outs, held, sems = refs[:count], refs[count:-count], refs[-count:-1], refs[-1]
    t_out, *outs = outs
    copies = [
        pltpu.make_async_copy(here, there, sems.at[i])
        for i, (here, there) in enumerate(zip(arguments, (t_out, *held)))
    ]
    for copy in copies:
        copy.start()
    for copy in copies:
        copy.wait()
    c, z, n_out = sizes.channels, sizes.slices, sizes.outputs
    k1_ref, b1_ref, k2_ref, b2_ref, k3_ref, b3_ref = held
    k1 = k1_ref[...].astype(F32)
    k3 = k3_ref[...].astype(F32)
    b1, b2 = b1_ref[...], b2_ref[...]

    k2 = [[k2_ref[a, b].astype(F32).T.astype(BF16) for b in range(3)] for a in range(3)]

    def first(ref, tap_of, tap_index):
        rows, lanes = ref.shape[0] // 3, ref.shape[1]
        for shift in range(3):
            lines = {(0, t): tile_lanes(k1[tap_index(shift, t)][None, :], lanes // c) for t in range(3)}
            ref[shift * rows : (shift + 1) * rows, :] = spread(tap_of, 0, (rows, lanes), lines)

    def last(shape, group_of, tap_of, tap_index, shift):
        lines = {
            (g, t): tile_lanes(k3[tap_index(shift, t)][g][None, :], shape[1] // c)
            for g in range(n_out)
            for t in range(3)
        }
        return spread(tap_of, group_of, shape, lines)

    def along_z(shift, t):
        return t, shift

    def along_x(shift, t):
        return shift, t

    w1, w2, w3, c1, c2 = outs[:5]
    shape = (w1.shape[0] // 3, w1.shape[1])
    first(w1, iota(shape, 0) // SUB - iota(shape, 1) // c, along_z)
    shape = (w3.shape[0] // 3, w3.shape[1])
    row = iota(shape, 0)
    for b in range(3):
        w2[b] = banded([k2[a][b] for a in range(3)], z + 2, z + 4, 0)
        w3[b * shape[0] : (b + 1) * shape[0], :] = last(
            shape, row // z, iota(shape, 1) // c - row % z, along_z, b
        )
    base = lax.axis_index("slab") * z
    for ref, bias, reach in ((c1, b1, 2), (c2, b2, 1)):
        where = base + iota(ref.shape, 1) // c - reach
        inside = (where >= 0) & (where < sizes.slabs * z)
        ref[...] = jnp.where(inside, tile_lanes(bias, ref.shape[1] // c), NEVER)

    for index, (image, one, two, out) in enumerate(sizes.kinds):
        w1, w2, w3, c1, c2 = outs[5 + 5 * index : 10 + 5 * index]
        shape = (w1.shape[0] // 3, w1.shape[1])
        first(w1, iota(shape, 0) % image[1] + image[0] - iota(shape, 1) // c - one[0] + 1, along_x)
        shape = (w3.shape[0] // 3, w3.shape[1])
        row = iota(shape, 0)
        tap = iota(shape, 1) // c + two[0] - row % SUB - out[0] + 1
        for a in range(3):
            w2[a] = banded([k2[a][b] for b in range(3)], two[1], one[1], one[0] - two[0] + 1)
            w3[a * shape[0] : (a + 1) * shape[0], :] = last(shape, row // SUB, tap, along_x, a)
        c1[...] = tile_lanes(b1, one[1])
        c2[...] = tile_lanes(b2, two[1])
    for g in range(n_out):
        outs[-1][g] = jnp.broadcast_to(b3_ref[0:1, g : g + 1], (SUB, sizes.rows))


def extend_kernel(own_ref, even_ref, odd_ref, out_ref):
    rows = own_ref.shape[2]
    before, after = before_and_after(even_ref[...], odd_ref[...], "row")
    out_ref[...] = jnp.concatenate([before[:, :, rows - 3 :], own_ref[...], after[:, :, :3]], axis=2)


def zero_groups(values, count, low, high):
    edge = count * SUB
    top, middle, bottom = values[:edge], values[edge:-edge], values[-edge:]
    if low.ndim:
        low, high = low[:edge], high[:edge]
    return jnp.concatenate([jnp.where(low, 0.0, top), middle, jnp.where(high, 0.0, bottom)], axis=0)


def taps(values, count):
    low, high = values.astype(BF16), values[SUB:].astype(BF16)
    return [low[:count], high[:count], low[2 * SUB : 2 * SUB + count]]


def pick(select, e):
    count = select.shape[1]
    return nt(select, jnp.concatenate([e[:, shift : shift + count] for shift in range(3)], axis=0))


def hidden_layers(picked, w1, w2, c1, c2, low, high):
    n2 = picked.shape[0] - 2 * SUB
    one = nn(picked.astype(BF16), w1[...])
    one = zero_groups(jnp.maximum(one + c1[...], 0.0), 2, low, high)
    two = sum(nn(tap, w2[i]) for i, tap in enumerate(taps(one, n2)))
    return zero_groups(jnp.maximum(two + c2[...], 0.0), 1, low, high)


def xy_kernel(sizes, e_ref, *refs):
    count = sum(1 for _ in sizes.kinds) * 5
    weights, (b3, out_ref, *hidden) = refs[:count], refs[count:]
    z, span = sizes.slices, sizes.span
    wide = sizes.rows + 6
    row = lax.axis_index("row")
    half = iota((2 * SUB, 1), 0) % SUB // z
    low = (row == 0) & (half == 0)
    high = (row == sizes.parts - 1) & (half == sizes.halves - 1)
    shape = ((span + 4) * SUB, sizes.rows + 4)
    wanted = iota(shape, 0) // SUB + iota(shape, 0) % SUB // z * span
    select = jnp.where(iota(shape, 1) == wanted, 1.0, 0.0).astype(BF16)
    for start, index in sizes.chunks:
        image = sizes.kinds[index][0]
        w1, w2, w3, c1, c2 = weights[5 * index : 5 * index + 5]
        low_col = start + image[0]
        e = e_ref[:, low_col : low_col + image[1], :].reshape(z * image[1], wide)
        picked = pick(select, e)
        same = iota(picked.shape, 1) // image[1] % z == iota(picked.shape, 0) % z
        picked = jnp.where(same, picked, 0.0)
        second = hidden_layers(picked, w1, w2, c1, c2, low, high)
        keep_hidden(hidden, second)
        runs = [
            (h * z + s, span if h < sizes.halves - 1 else span + SUB)
            for s in range(z)
            for h in range(sizes.halves)
        ]
        total = last_layer(w3, gather_hidden(hidden, runs, second.shape[1]))
        here = slice(start, start + SUB)
        for s in range(z):
            xy = [
                total[g * SUB : (g + 1) * SUB, s * sizes.slot : s * sizes.slot + sizes.rows] + b3[g] for g in range(3)
            ]
            out_ref[0, s, here, :] = b3[0]
            out_ref[1, s, here, :] = 0.5 * (xy[0] + b3[1])
            out_ref[2, s, here, :] = xy[1]
            out_ref[3, s, here, :] = 0.5 * (xy[2] + b3[2])


def yz_kernel(sizes, e_ref, round_2, round_1, round_0, base_ref, w1, w2, w3, c1, c2, out_ref, turned):
    z = sizes.slices
    wide = sizes.rows + 6
    row = lax.axis_index("row")
    low, high = row == 0, row == sizes.parts - 1
    slab = lax.axis_index("slab")
    early = lax.axis_index("row") < EARLY
    swapped = [ref[...] for ref in (round_0, round_1, round_2)]
    even = jnp.where(early & (slab < 2), swapped[0], swapped[1])
    even = jnp.where(early & (slab >= 2) & (slab < 4), swapped[2], even)
    odd = jnp.where(early & (slab >= 1) & (slab < 3), swapped[1], swapped[0])
    before, after = before_and_after(even, odd, "slab")
    block = jnp.concatenate([before[z - 3 :], e_ref[...], after[:3]], axis=0)
    shape = ((sizes.rows + 4) * SUB, sizes.rows + 4)
    select = jnp.where(iota(shape, 1) == iota(shape, 0) // SUB, 1.0, 0.0).astype(BF16)
    for start in range(0, sizes.cols, SUB):
        e = block[:, start : start + SUB, :].reshape((z + 6) * SUB, wide)
        flat = e.astype(F32).T
        count = sizes.rows + 4
        flat = jnp.concatenate([flat[shift : shift + count] for shift in range(3)], axis=1)
        picked = jnp.broadcast_to(flat[:, None, :], (count, SUB, flat.shape[1])).reshape(count * SUB, flat.shape[1])
        same = iota(picked.shape, 1) % SUB == iota(picked.shape, 0) % SUB
        picked = jnp.where(same, picked, 0.0)
        two = hidden_layers(picked, w1, w2, c1, c2, low, high)
        lanes = two.shape[1]
        tall = jnp.concatenate([two, jnp.zeros((sizes.slot * SUB - two.shape[0], lanes), F32)], axis=0)
        tall = tall.reshape(sizes.slot, SUB, lanes).transpose(1, 0, 2).reshape(SUB * sizes.slot, lanes)
        total = last_layer(w3, tall.astype(BF16))
        rest = jnp.zeros((total.shape[0], LANES - sizes.rows), F32)
        for x in range(SUB):
            piece = total[:, x * sizes.slot : x * sizes.slot + sizes.rows]
            turned[pl.ds(x, total.shape[0], stride=SUB), :] = jnp.concatenate([piece, rest], axis=1)
        here = slice(start, start + SUB)
        for s in range(z):
            yz = [turned[(g * z + s) * SUB : (g * z + s + 1) * SUB, : sizes.rows] for g in range(3)]
            out_ref[0, s, here, :] = base_ref[0, s, here, :] + yz[0]
            out_ref[1, s, here, :] = base_ref[1, s, here, :] + 0.5 * yz[1]
            out_ref[2, s, here, :] = base_ref[2, s, here, :]
            out_ref[3, s, here, :] = base_ref[3, s, here, :] + 0.5 * yz[2]


def call(kernel, name, outs, args, scratch=(), flops=0, space=pltpu.VMEM):
    single = not isinstance(outs, list)
    shapes = [jax.ShapeDtypeStruct(shape, kind) for shape, kind in ([outs] if single else outs)]
    return pl.pallas_call(
        kernel,
        name=name,
        out_shape=shapes[0] if single else shapes,
        in_specs=[pl.BlockSpec(memory_space=space)] * len(args),
        scratch_shapes=scratch,
        compiler_params=pltpu.CompilerParams(vmem_limit_bytes=LIMIT),
        cost_estimate=pl.CostEstimate(flops=flops, bytes_accessed=1 << 20, transcendentals=0),
    )(*args)


def local(image, first_kernel, first_bias, middle_kernel, middle_bias, last_kernel, last_bias):
    slices, rows, cols = image.shape
    channels, outputs = first_kernel.shape[2], last_kernel.shape[2]
    sizes = Sizes(slices, rows, cols, channels, outputs, lax.axis_size("slab"), lax.axis_size("row"))
    t = image.transpose(0, 2, 1)
    even, odd = swap_rows(t, 0), swap_rows(t, 1)
    parameters = (
        first_kernel.reshape(3, 3, channels),
        first_bias.reshape(1, channels),
        middle_kernel,
        middle_bias.reshape(1, channels),
        last_kernel,
        last_bias.reshape(1, outputs),
    )
    own, *weights = call(
        functools.partial(prepare_kernel, sizes),
        "prepare",
        [(t.shape, BF16), *sizes.weight_shapes()],
        [pltpu.with_memory_space_constraint(p, pltpu.HBM) for p in (t, *parameters)],
        [pltpu.VMEM(p.shape, p.dtype) for p in parameters] + [pltpu.SemaphoreType.DMA((7,))],
        flops=1 << 20,
        space=pltpu.HBM,
    )
    wide = rows + 6
    e = call(extend_kernel, "extend", ((slices, cols, wide), BF16), (own, even, odd))
    swapped = [swap_slabs(e, turn_of) for turn_of in (2, 1, 0)]
    lanes = max(kind[2][1] for kind in sizes.kinds) * channels
    xy_hidden = pltpu.VMEM(((sizes.span + SUB) * SUB, LANES), F32)
    base = call(
        functools.partial(xy_kernel, sizes),
        "xy",
        ((outputs + 1, slices, cols, rows), F32),
        (e, *weights[5:]),
        [xy_hidden] * pl.cdiv(lanes, LANES),
        flops=1 << 28,
    )
    flows = call(
        functools.partial(yz_kernel, sizes),
        "yz",
        ((outputs + 1, slices, cols, rows), F32),
        (e, *swapped, base, *weights[:5]),
        [pltpu.VMEM((sizes.padded * SUB, LANES), F32)],
        flops=1 << 28,
    )
    return flows.transpose(0, 1, 3, 2)


def solution(mesh):
    placed = (P("slab", "row", None), P(), P(), P(), P(), P(), P())
    return jax.shard_map(
        local, mesh=mesh, in_specs=placed, out_specs=P(None, "slab", "row", None), check_vma=False
    )
```

```python
import functools

import jax
import jax.numpy as jnp
from jax import lax
from jax.experimental import pallas as pl
from jax.experimental.pallas import tpu as pltpu
from jax.sharding import PartitionSpec as P

SUB = 8
LANES = 128
NEVER = -3.0e38
LIMIT = 12 << 20
F32 = jnp.float32
BF16 = jnp.bfloat16


def matching(count, parity):
    partner = {}
    for left in range(parity, count - 1, 2):
        partner[left] = left + 1
        partner[left + 1] = left
    return partner


def swap_rows(values, parity):
    count = lax.axis_size("row")
    partner = matching(count, parity)
    ends = [i for i in range(count) if i not in partner]
    for here, there in zip(ends, reversed(ends)):
        partner[here] = there
    return lax.ppermute(values, "row", sorted(partner.items()))


EARLY = 2


def slab_rounds(slabs, row):
    borders = list(range(slabs - 1))
    if row < EARLY:
        return [borders[:1] + borders[3::2], borders[1:2] + borders[4::2], borders[2:3]]
    return [borders[1::2], borders[::2], []]


def swap_slabs(values, turn_of):
    slabs, rows = lax.axis_size("slab"), lax.axis_size("row")
    across = matching(rows, 0)
    pairs = []
    for r in range(rows):
        partner = {}
        for border in slab_rounds(slabs, r)[turn_of]:
            partner[border], partner[border + 1] = border + 1, border
        for s in range(slabs):
            there = (partner[s], r) if s in partner else (s, across.get(r, r))
            pairs.append((s * rows + r, there[0] * rows + there[1]))
    return lax.ppermute(values, ("slab", "row"), sorted(pairs))


def before_and_after(even, odd, axis):
    here, count = lax.axis_index(axis), lax.axis_size(axis)
    low = here % 2 == 0
    before = jnp.where(low, odd, even)
    after = jnp.where(low, even, odd)
    before = jnp.where(here > 0, before, jnp.zeros_like(before))
    after = jnp.where(here < count - 1, after, jnp.zeros_like(after))
    return before, after


def tile_lanes(row, count):
    return jnp.concatenate([row] * count, axis=1)


def iota(shape, dim):
    return lax.broadcasted_iota(jnp.int32, shape, dim)


def nn(left, right):
    return lax.dot_general(left, right, (((1,), (0,)), ((), ())), preferred_element_type=F32)


def nt(left, right):
    return lax.dot_general(left, right, (((1,), (1,)), ((), ())), preferred_element_type=F32)


def last_layer(w3, hidden):
    every = nt(w3[...], hidden)
    count, lanes = every.shape[0] // 3, every.shape[1] - SUB
    return sum(every[i * count : (i + 1) * count, i : i + lanes] for i in range(3))


class Sizes:
    def __init__(self, slices, rows, cols, channels, outputs, slabs, parts):
        self.slices, self.rows, self.cols = slices, rows, cols
        self.channels, self.outputs = channels, outputs
        self.slabs, self.parts = slabs, parts
        assert slices >= 3 and SUB % slices == 0
        self.halves = SUB // slices
        assert rows % self.halves == 0 and cols % SUB == 0
        self.span = rows // self.halves
        self.padded = -(-outputs * slices // SUB) * SUB
        self.slot = rows + SUB
        self.chunks = []
        self.kinds = []
        for start in range(0, cols, SUB):
            ranges = []
            for reach in (3, 2, 1, 0):
                low = max(0, start - reach)
                ranges.append((low - start, min(cols, start + SUB + reach) - low))
            kind = tuple(ranges)
            if kind not in self.kinds:
                self.kinds.append(kind)
            self.chunks.append((start, self.kinds.index(kind)))

    def weight_shapes(self):
        c, z = self.channels, self.slices
        shapes = [
            ((3 * (z + 6) * SUB, (z + 4) * c), BF16),
            ((3, (z + 4) * c, (z + 2) * c), BF16),
            ((3 * self.padded, (z + 2) * c), BF16),
            ((1, (z + 4) * c), F32),
            ((1, (z + 2) * c), F32),
        ]
        for image, one, two, _ in self.kinds:
            shapes += [
                ((3 * z * image[1], one[1] * c), BF16),
                ((3, one[1] * c, two[1] * c), BF16),
                ((3 * self.outputs * SUB, two[1] * c), BF16),
                ((1, one[1] * c), F32),
                ((1, two[1] * c), F32),
            ]
        return shapes + [((self.outputs, SUB, self.rows), F32)]


def banded(blocks, out_count, in_count, offset):
    zero = jnp.zeros_like(blocks[0])
    lines = []
    for inner in range(in_count):
        line = []
        for out in range(out_count):
            tap = inner - out + offset
            line.append(blocks[tap] if 0 <= tap < 3 else zero)
        lines.append(jnp.concatenate(line, axis=1))
    return jnp.concatenate(lines, axis=0)


def spread(tap_of, group_of, shape, lines):
    total = jnp.zeros(shape, F32)
    for (group, tap), line in lines.items():
        total = jnp.where((tap_of == tap) & (group_of == group), line, total)
    return total.astype(BF16)


def prepare_kernel(sizes, *refs):
    count = 7
    arguments, outs, held, sems = refs[:count], refs[count:-count], refs[-count:-1], refs[-1]
    t_out, *outs = outs
    copies = [
        pltpu.make_async_copy(here, there, sems.at[i])
        for i, (here, there) in enumerate(zip(arguments, (t_out, *held)))
    ]
    for copy in copies:
        copy.start()
    for copy in copies:
        copy.wait()
    c, z, n_out = sizes.channels, sizes.slices, sizes.outputs
    k1_ref, b1_ref, k2_ref, b2_ref, k3_ref, b3_ref = held
    k1 = k1_ref[...].astype(F32)
    k3 = k3_ref[...].astype(F32)
    b1, b2 = b1_ref[...], b2_ref[...]

    k2 = [[k2_ref[a, b].astype(F32).T.astype(BF16) for b in range(3)] for a in range(3)]

    def first(ref, tap_of, tap_index):
        rows, lanes = ref.shape[0] // 3, ref.shape[1]
        for shift in range(3):
            lines = {(0, t): tile_lanes(k1[tap_index(shift, t)][None, :], lanes // c) for t in range(3)}
            ref[shift * rows : (shift + 1) * rows, :] = spread(tap_of, 0, (rows, lanes), lines)

    def last(shape, group_of, tap_of, tap_index, shift):
        lines = {
            (g, t): tile_lanes(k3[tap_index(shift, t)][g][None, :], shape[1] // c)
            for g in range(n_out)
            for t in range(3)
        }
        return spread(tap_of, group_of, shape, lines)

    def along_z(shift, t):
        return t, shift

    def along_x(shift, t):
        return shift, t

    w1, w2, w3, c1, c2 = outs[:5]
    shape = (w1.shape[0] // 3, w1.shape[1])
    first(w1, iota(shape, 0) // SUB - iota(shape, 1) // c, along_z)
    shape = (w3.shape[0] // 3, w3.shape[1])
    row = iota(shape, 0)
    for b in range(3):
        w2[b] = banded([k2[a][b] for a in range(3)], z + 2, z + 4, 0)
        w3[b * shape[0] : (b + 1) * shape[0], :] = last(
            shape, row // z, iota(shape, 1) // c - row % z, along_z, b
        )
    base = lax.axis_index("slab") * z
    for ref, bias, reach in ((c1, b1, 2), (c2, b2, 1)):
        where = base + iota(ref.shape, 1) // c - reach
        inside = (where >= 0) & (where < sizes.slabs * z)
        ref[...] = jnp.where(inside, tile_lanes(bias, ref.shape[1] // c), NEVER)

    for index, (image, one, two, out) in enumerate(sizes.kinds):
        w1, w2, w3, c1, c2 = outs[5 + 5 * index : 10 + 5 * index]
        shape = (w1.shape[0] // 3, w1.shape[1])
        first(w1, iota(shape, 0) % image[1] + image[0] - iota(shape, 1) // c - one[0] + 1, along_x)
        shape = (w3.shape[0] // 3, w3.shape[1])
        row = iota(shape, 0)
        tap = iota(shape, 1) // c + two[0] - row % SUB - out[0] + 1
        for a in range(3):
            w2[a] = banded([k2[a][b] for b in range(3)], two[1], one[1], one[0] - two[0] + 1)
            w3[a * shape[0] : (a + 1) * shape[0], :] = last(shape, row // SUB, tap, along_x, a)
        c1[...] = tile_lanes(b1, one[1])
        c2[...] = tile_lanes(b2, two[1])
    for g in range(n_out):
        outs[-1][g] = jnp.broadcast_to(b3_ref[0:1, g : g + 1], (SUB, sizes.rows))


def extend_kernel(own_ref, even_ref, odd_ref, out_ref):
    rows = own_ref.shape[2]
    before, after = before_and_after(even_ref[...], odd_ref[...], "row")
    out_ref[...] = jnp.concatenate([before[:, :, rows - 3 :], own_ref[...], after[:, :, :3]], axis=2)


def zero_groups(values, count, low, high):
    edge = count * SUB
    top, middle, bottom = values[:edge], values[edge:-edge], values[-edge:]
    if low.ndim:
        low, high = low[:edge], high[:edge]
    return jnp.concatenate([jnp.where(low, 0.0, top), middle, jnp.where(high, 0.0, bottom)], axis=0)


def taps(values, count):
    low, high = values.astype(BF16), values[SUB:].astype(BF16)
    return [low[:count], high[:count], low[2 * SUB : 2 * SUB + count]]


def pick(select, e):
    count = select.shape[1]
    return nt(select, jnp.concatenate([e[:, shift : shift + count] for shift in range(3)], axis=0))


def hidden_layers(picked, w1, w2, c1, c2, low, high):
    n2 = picked.shape[0] - 2 * SUB
    one = nn(picked.astype(BF16), w1[...])
    one = zero_groups(jnp.maximum(one + c1[...], 0.0), 2, low, high)
    two = sum(nn(tap, w2[i]) for i, tap in enumerate(taps(one, n2)))
    return zero_groups(jnp.maximum(two + c2[...], 0.0), 1, low, high)


def xy_kernel(sizes, e_ref, *refs):
    count = sum(1 for _ in sizes.kinds) * 5
    weights, (b3, out_ref) = refs[:count], refs[count:]
    z, span = sizes.slices, sizes.span
    wide = sizes.rows + 6
    row = lax.axis_index("row")
    half = iota((2 * SUB, 1), 0) % SUB // z
    low = (row == 0) & (half == 0)
    high = (row == sizes.parts - 1) & (half == sizes.halves - 1)
    shape = ((span + 4) * SUB, sizes.rows + 4)
    wanted = iota(shape, 0) // SUB + iota(shape, 0) % SUB // z * span
    select = jnp.where(iota(shape, 1) == wanted, 1.0, 0.0).astype(BF16)
    for start, index in sizes.chunks:
        image = sizes.kinds[index][0]
        w1, w2, w3, c1, c2 = weights[5 * index : 5 * index + 5]
        low_col = start + image[0]
        e = e_ref[:, low_col : low_col + image[1], :].reshape(z * image[1], wide)
        picked = pick(select, e)
        same = iota(picked.shape, 1) // image[1] % z == iota(picked.shape, 0) % z
        picked = jnp.where(same, picked, 0.0)
        second = hidden_layers(picked, w1, w2, c1, c2, low, high)
        lanes, last = second.shape[1], sizes.halves - 1
        tall = jnp.concatenate([second, jnp.zeros((6 * SUB, lanes), F32)], axis=0)
        tall = tall.reshape(-1, SUB, lanes).transpose(1, 0, 2)
        parts = [
            tall[h * z + s, : span if h < last else span + SUB] for s in range(z) for h in range(sizes.halves)
        ]
        total = last_layer(w3, jnp.concatenate(parts, axis=0).astype(BF16))
        here = slice(start, start + SUB)
        for s in range(z):
            xy = [
                total[g * SUB : (g + 1) * SUB, s * sizes.slot : s * sizes.slot + sizes.rows] + b3[g] for g in range(3)
            ]
            out_ref[0, s, here, :] = b3[0]
            out_ref[1, s, here, :] = 0.5 * (xy[0] + b3[1])
            out_ref[2, s, here, :] = xy[1]
            out_ref[3, s, here, :] = 0.5 * (xy[2] + b3[2])


def yz_kernel(sizes, e_ref, round_2, round_1, round_0, base_ref, w1, w2, w3, c1, c2, out_ref, turned):
    z = sizes.slices
    wide = sizes.rows + 6
    row = lax.axis_index("row")
    low, high = row == 0, row == sizes.parts - 1
    slab = lax.axis_index("slab")
    early = lax.axis_index("row") < EARLY
    swapped = [ref[...] for ref in (round_0, round_1, round_2)]
    even = jnp.where(early & (slab < 2), swapped[0], swapped[1])
    even = jnp.where(early & (slab >= 2) & (slab < 4), swapped[2], even)
    odd = jnp.where(early & (slab >= 1) & (slab < 3), swapped[1], swapped[0])
    before, after = before_and_after(even, odd, "slab")
    block = jnp.concatenate([before[z - 3 :], e_ref[...], after[:3]], axis=0)
    shape = ((sizes.rows + 4) * SUB, sizes.rows + 4)
    select = jnp.where(iota(shape, 1) == iota(shape, 0) // SUB, 1.0, 0.0).astype(BF16)
    for start in range(0, sizes.cols, SUB):
        e = block[:, start : start + SUB, :].reshape((z + 6) * SUB, wide)
        flat = e.astype(F32).T
        count = sizes.rows + 4
        flat = jnp.concatenate([flat[shift : shift + count] for shift in range(3)], axis=1)
        picked = jnp.broadcast_to(flat[:, None, :], (count, SUB, flat.shape[1])).reshape(count * SUB, flat.shape[1])
        same = iota(picked.shape, 1) % SUB == iota(picked.shape, 0) % SUB
        picked = jnp.where(same, picked, 0.0)
        two = hidden_layers(picked, w1, w2, c1, c2, low, high)
        lanes = two.shape[1]
        tall = jnp.concatenate([two, jnp.zeros((sizes.slot * SUB - two.shape[0], lanes), F32)], axis=0)
        tall = tall.reshape(sizes.slot, SUB, lanes).transpose(1, 0, 2).reshape(SUB * sizes.slot, lanes)
        total = last_layer(w3, tall.astype(BF16))
        rest = jnp.zeros((total.shape[0], LANES - sizes.rows), F32)
        for x in range(SUB):
            piece = total[:, x * sizes.slot : x * sizes.slot + sizes.rows]
            turned[pl.ds(x, total.shape[0], stride=SUB), :] = jnp.concatenate([piece, rest], axis=1)
        here = slice(start, start + SUB)
        for s in range(z):
            yz = [turned[(g * z + s) * SUB : (g * z + s + 1) * SUB, : sizes.rows] for g in range(3)]
            out_ref[0, s, here, :] = base_ref[0, s, here, :] + yz[0]
            out_ref[1, s, here, :] = base_ref[1, s, here, :] + 0.5 * yz[1]
            out_ref[2, s, here, :] = base_ref[2, s, here, :]
            out_ref[3, s, here, :] = base_ref[3, s, here, :] + 0.5 * yz[2]


def call(kernel, name, outs, args, scratch=(), flops=0, space=pltpu.VMEM):
    single = not isinstance(outs, list)
    shapes = [jax.ShapeDtypeStruct(shape, kind) for shape, kind in ([outs] if single else outs)]
    return pl.pallas_call(
        kernel,
        name=name,
        out_shape=shapes[0] if single else shapes,
        in_specs=[pl.BlockSpec(memory_space=space)] * len(args),
        scratch_shapes=scratch,
        compiler_params=pltpu.CompilerParams(vmem_limit_bytes=LIMIT),
        cost_estimate=pl.CostEstimate(flops=flops, bytes_accessed=1 << 20, transcendentals=0),
    )(*args)


def local(image, first_kernel, first_bias, middle_kernel, middle_bias, last_kernel, last_bias):
    slices, rows, cols = image.shape
    channels, outputs = first_kernel.shape[2], last_kernel.shape[2]
    sizes = Sizes(slices, rows, cols, channels, outputs, lax.axis_size("slab"), lax.axis_size("row"))
    t = image.transpose(0, 2, 1)
    even, odd = swap_rows(t, 0), swap_rows(t, 1)
    parameters = (
        first_kernel.reshape(3, 3, channels),
        first_bias.reshape(1, channels),
        middle_kernel,
        middle_bias.reshape(1, channels),
        last_kernel,
        last_bias.reshape(1, outputs),
    )
    own, *weights = call(
        functools.partial(prepare_kernel, sizes),
        "prepare",
        [(t.shape, BF16), *sizes.weight_shapes()],
        [pltpu.with_memory_space_constraint(p, pltpu.HBM) for p in (t, *parameters)],
        [pltpu.VMEM(p.shape, p.dtype) for p in parameters] + [pltpu.SemaphoreType.DMA((7,))],
        flops=1 << 20,
        space=pltpu.HBM,
    )
    wide = rows + 6
    e = call(extend_kernel, "extend", ((slices, cols, wide), BF16), (own, even, odd))
    swapped = [swap_slabs(e, turn_of) for turn_of in (2, 1, 0)]
    base = call(
        functools.partial(xy_kernel, sizes),
        "xy",
        ((outputs + 1, slices, cols, rows), F32),
        (e, *weights[5:]),
        flops=1 << 28,
    )
    flows = call(
        functools.partial(yz_kernel, sizes),
        "yz",
        ((outputs + 1, slices, cols, rows), F32),
        (e, *swapped, base, *weights[:5]),
        [pltpu.VMEM((sizes.padded * SUB, LANES), F32)],
        flops=1 << 28,
    )
    return flows.transpose(0, 1, 3, 2)


def solution(mesh):
    placed = (P("slab", "row", None), P(), P(), P(), P(), P(), P())
    return jax.shard_map(
        local, mesh=mesh, in_specs=placed, out_specs=P(None, "slab", "row", None), check_vma=False
    )
```

```python
import functools

import jax
import jax.numpy as jnp
from jax import lax
from jax.experimental import pallas as pl
from jax.experimental.pallas import tpu as pltpu
from jax.sharding import PartitionSpec as P

SUB = 8
LANES = 128
NEVER = -3.0e38
LIMIT = 12 << 20
F32 = jnp.float32
BF16 = jnp.bfloat16


def matching(count, parity):
    partner = {}
    for left in range(parity, count - 1, 2):
        partner[left] = left + 1
        partner[left + 1] = left
    return partner


def swap_rows(values, parity):
    count = lax.axis_size("row")
    partner = matching(count, parity)
    ends = [i for i in range(count) if i not in partner]
    for here, there in zip(ends, reversed(ends)):
        partner[here] = there
    return lax.ppermute(values, "row", sorted(partner.items()))


EARLY = 2


def slab_rounds(slabs, row):
    borders = list(range(slabs - 1))
    if row < EARLY:
        return [borders[:1] + borders[3::2], borders[1:2] + borders[4::2], borders[2:3]]
    return [borders[1::2], borders[::2], []]


def swap_slabs(values, turn_of):
    slabs, rows = lax.axis_size("slab"), lax.axis_size("row")
    across = matching(rows, 0)
    pairs = []
    for r in range(rows):
        partner = {}
        for border in slab_rounds(slabs, r)[turn_of]:
            partner[border], partner[border + 1] = border + 1, border
        for s in range(slabs):
            there = (partner[s], r) if s in partner else (s, across.get(r, r))
            pairs.append((s * rows + r, there[0] * rows + there[1]))
    return lax.ppermute(values, ("slab", "row"), sorted(pairs))


def before_and_after(even, odd, axis):
    here, count = lax.axis_index(axis), lax.axis_size(axis)
    low = here % 2 == 0
    before = jnp.where(low, odd, even)
    after = jnp.where(low, even, odd)
    before = jnp.where(here > 0, before, jnp.zeros_like(before))
    after = jnp.where(here < count - 1, after, jnp.zeros_like(after))
    return before, after


def tile_lanes(row, count):
    return jnp.concatenate([row] * count, axis=1)


def iota(shape, dim):
    return lax.broadcasted_iota(jnp.int32, shape, dim)


def nn(left, right):
    return lax.dot_general(left, right, (((1,), (0,)), ((), ())), preferred_element_type=F32)


def nt(left, right):
    return lax.dot_general(left, right, (((1,), (1,)), ((), ())), preferred_element_type=F32)


def keep_hidden(scratch, values):
    for i in range(0, values.shape[1], LANES):
        piece = values[:, i : i + LANES]
        scratch[i // LANES][: piece.shape[0], : piece.shape[1]] = piece


def gather_hidden(scratch, runs, lanes):
    columns = []
    for i in range(0, lanes, LANES):
        parts = [scratch[i // LANES][pl.ds(start, count, stride=SUB), :] for start, count in runs]
        columns.append(jnp.concatenate(parts, axis=0).astype(BF16)[:, : lanes - i])
    return jnp.concatenate(columns, axis=1)


def last_layer(w3, hidden):
    every = nt(w3[...], hidden)
    count, lanes = every.shape[0] // 3, every.shape[1] - SUB
    return sum(every[i * count : (i + 1) * count, i : i + lanes] for i in range(3))


class Sizes:
    def __init__(self, slices, rows, cols, channels, outputs, slabs, parts):
        self.slices, self.rows, self.cols = slices, rows, cols
        self.channels, self.outputs = channels, outputs
        self.slabs, self.parts = slabs, parts
        assert slices >= 3 and SUB % slices == 0
        self.halves = SUB // slices
        assert rows % self.halves == 0 and cols % SUB == 0
        self.span = rows // self.halves
        self.padded = -(-outputs * slices // SUB) * SUB
        self.slot = rows + SUB
        self.chunks = []
        self.kinds = []
        for start in range(0, cols, SUB):
            ranges = []
            for reach in (3, 2, 1, 0):
                low = max(0, start - reach)
                ranges.append((low - start, min(cols, start + SUB + reach) - low))
            kind = tuple(ranges)
            if kind not in self.kinds:
                self.kinds.append(kind)
            self.chunks.append((start, self.kinds.index(kind)))

    def weight_shapes(self):
        c, z = self.channels, self.slices
        shapes = [
            ((3 * (z + 6) * SUB, (z + 4) * c), BF16),
            ((3, (z + 4) * c, (z + 2) * c), BF16),
            ((3 * self.padded, (z + 2) * c), BF16),
            ((1, (z + 4) * c), F32),
            ((1, (z + 2) * c), F32),
        ]
        for image, one, two, _ in self.kinds:
            shapes += [
                ((3 * z * image[1], one[1] * c), BF16),
                ((3, one[1] * c, two[1] * c), BF16),
                ((3 * self.outputs * SUB, two[1] * c), BF16),
                ((1, one[1] * c), F32),
                ((1, two[1] * c), F32),
            ]
        return shapes + [((self.outputs, SUB, self.rows), F32)]


def banded(blocks, out_count, in_count, offset):
    zero = jnp.zeros_like(blocks[0])
    lines = []
    for inner in range(in_count):
        line = []
        for out in range(out_count):
            tap = inner - out + offset
            line.append(blocks[tap] if 0 <= tap < 3 else zero)
        lines.append(jnp.concatenate(line, axis=1))
    return jnp.concatenate(lines, axis=0)


def spread(tap_of, group_of, shape, lines):
    total = jnp.zeros(shape, F32)
    for (group, tap), line in lines.items():
        total = jnp.where((tap_of == tap) & (group_of == group), line, total)
    return total.astype(BF16)


def prepare_kernel(sizes, *refs):
    count = 7
    arguments, outs, held, sems = refs[:count], refs[count:-count], refs[-count:-1], refs[-1]
    t_out, *outs = outs
    copies = [
        pltpu.make_async_copy(here, there, sems.at[i])
        for i, (here, there) in enumerate(zip(arguments, (t_out, *held)))
    ]
    for copy in copies:
        copy.start()
    for copy in copies:
        copy.wait()
    c, z, n_out = sizes.channels, sizes.slices, sizes.outputs
    k1_ref, b1_ref, k2_ref, b2_ref, k3_ref, b3_ref = held
    k1 = k1_ref[...].astype(F32)
    k3 = k3_ref[...].astype(F32)
    b1, b2 = b1_ref[...], b2_ref[...]

    k2 = [[k2_ref[a, b].astype(F32).T.astype(BF16) for b in range(3)] for a in range(3)]

    def first(ref, tap_of, tap_index):
        rows, lanes = ref.shape[0] // 3, ref.shape[1]
        for shift in range(3):
            lines = {(0, t): tile_lanes(k1[tap_index(shift, t)][None, :], lanes // c) for t in range(3)}
            ref[shift * rows : (shift + 1) * rows, :] = spread(tap_of, 0, (rows, lanes), lines)

    def last(shape, group_of, tap_of, tap_index, shift):
        lines = {
            (g, t): tile_lanes(k3[tap_index(shift, t)][g][None, :], shape[1] // c)
            for g in range(n_out)
            for t in range(3)
        }
        return spread(tap_of, group_of, shape, lines)

    def along_z(shift, t):
        return t, shift

    def along_x(shift, t):
        return shift, t

    w1, w2, w3, c1, c2 = outs[:5]
    shape = (w1.shape[0] // 3, w1.shape[1])
    first(w1, iota(shape, 0) // SUB - iota(shape, 1) // c, along_z)
    shape = (w3.shape[0] // 3, w3.shape[1])
    row = iota(shape, 0)
    for b in range(3):
        w2[b] = banded([k2[a][b] for a in range(3)], z + 2, z + 4, 0)
        w3[b * shape[0] : (b + 1) * shape[0], :] = last(
            shape, row // z, iota(shape, 1) // c - row % z, along_z, b
        )
    base = lax.axis_index("slab") * z
    for ref, bias, reach in ((c1, b1, 2), (c2, b2, 1)):
        where = base + iota(ref.shape, 1) // c - reach
        inside = (where >= 0) & (where < sizes.slabs * z)
        ref[...] = jnp.where(inside, tile_lanes(bias, ref.shape[1] // c), NEVER)

    for index, (image, one, two, out) in enumerate(sizes.kinds):
        w1, w2, w3, c1, c2 = outs[5 + 5 * index : 10 + 5 * index]
        shape = (w1.shape[0] // 3, w1.shape[1])
        first(w1, iota(shape, 0) % image[1] + image[0] - iota(shape, 1) // c - one[0] + 1, along_x)
        shape = (w3.shape[0] // 3, w3.shape[1])
        row = iota(shape, 0)
        tap = iota(shape, 1) // c + two[0] - row % SUB - out[0] + 1
        for a in range(3):
            w2[a] = banded([k2[a][b] for b in range(3)], two[1], one[1], one[0] - two[0] + 1)
            w3[a * shape[0] : (a + 1) * shape[0], :] = last(shape, row // SUB, tap, along_x, a)
        c1[...] = tile_lanes(b1, one[1])
        c2[...] = tile_lanes(b2, two[1])
    for g in range(n_out):
        outs[-1][g] = jnp.broadcast_to(b3_ref[0:1, g : g + 1], (SUB, sizes.rows))


def extend_kernel(own_ref, even_ref, odd_ref, out_ref):
    rows = own_ref.shape[2]
    here, count = lax.axis_index("row"), lax.axis_size("row")
    low = here % 2 == 0
    edge = jnp.concatenate([jnp.where(low, odd_ref[...], even_ref[...])[:, :, rows - 3 :], own_ref[...]], axis=2)
    every = jnp.concatenate([edge, jnp.where(low, even_ref[...], odd_ref[...])[:, :, :3]], axis=2)
    lane = iota(every.shape, 2)
    first = jnp.where(here > 0, 0, 3)
    final = jnp.where(here < count - 1, rows + 6, rows + 3)
    out_ref[...] = jnp.where((lane >= first) & (lane < final), every.astype(F32), 0.0).astype(BF16)


def zero_groups(values, count, low, high):
    edge = count * SUB
    top, middle, bottom = values[:edge], values[edge:-edge], values[-edge:]
    if low.ndim:
        low, high = low[:edge], high[:edge]
    return jnp.concatenate([jnp.where(low, 0.0, top), middle, jnp.where(high, 0.0, bottom)], axis=0)


def taps(values, count):
    low, high = values.astype(BF16), values[SUB:].astype(BF16)
    return [low[:count], high[:count], low[2 * SUB : 2 * SUB + count]]


def pick(select, e):
    count = select.shape[1]
    return nt(select, jnp.concatenate([e[:, shift : shift + count] for shift in range(3)], axis=0))


def hidden_layers(picked, w1, w2, c1, c2, low, high):
    n2 = picked.shape[0] - 2 * SUB
    one = nn(picked.astype(BF16), w1[...])
    one = zero_groups(jnp.maximum(one + c1[...], 0.0), 2, low, high)
    two = sum(nn(tap, w2[i]) for i, tap in enumerate(taps(one, n2)))
    return zero_groups(jnp.maximum(two + c2[...], 0.0), 1, low, high)


def xy_kernel(sizes, e_ref, *refs):
    count = sum(1 for _ in sizes.kinds) * 5
    weights, (b3, out_ref, *hidden) = refs[:count], refs[count:]
    z, span = sizes.slices, sizes.span
    wide = sizes.rows + 6
    row = lax.axis_index("row")
    half = iota((2 * SUB, 1), 0) % SUB // z
    low = (row == 0) & (half == 0)
    high = (row == sizes.parts - 1) & (half == sizes.halves - 1)
    shape = ((span + 4) * SUB, sizes.rows + 4)
    wanted = iota(shape, 0) // SUB + iota(shape, 0) % SUB // z * span
    select = jnp.where(iota(shape, 1) == wanted, 1.0, 0.0).astype(BF16)
    for start, index in sizes.chunks:
        image = sizes.kinds[index][0]
        w1, w2, w3, c1, c2 = weights[5 * index : 5 * index + 5]
        low_col = start + image[0]
        e = e_ref[:, low_col : low_col + image[1], :].reshape(z * image[1], wide)
        picked = pick(select, e)
        same = iota(picked.shape, 1) // image[1] % z == iota(picked.shape, 0) % z
        picked = jnp.where(same, picked, 0.0)
        second = hidden_layers(picked, w1, w2, c1, c2, low, high)
        keep_hidden(hidden, second)
        runs = [
            (h * z + s, span if h < sizes.halves - 1 else span + SUB)
            for s in range(z)
            for h in range(sizes.halves)
        ]
        total = last_layer(w3, gather_hidden(hidden, runs, second.shape[1]))
        here = slice(start, start + SUB)
        for s in range(z):
            xy = [
                total[g * SUB : (g + 1) * SUB, s * sizes.slot : s * sizes.slot + sizes.rows] + b3[g] for g in range(3)
            ]
            out_ref[0, s, here, :] = b3[0]
            out_ref[1, s, here, :] = 0.5 * (xy[0] + b3[1])
            out_ref[2, s, here, :] = xy[1]
            out_ref[3, s, here, :] = 0.5 * (xy[2] + b3[2])


def yz_kernel(sizes, e_ref, round_2, round_1, round_0, base_ref, w1, w2, w3, c1, c2, out_ref, turned):
    z = sizes.slices
    wide = sizes.rows + 6
    row = lax.axis_index("row")
    low, high = row == 0, row == sizes.parts - 1
    slab = lax.axis_index("slab")
    early = lax.axis_index("row") < EARLY
    swapped = [ref[...] for ref in (round_0, round_1, round_2)]
    even = jnp.where(early & (slab < 2), swapped[0], swapped[1])
    even = jnp.where(early & (slab >= 2) & (slab < 4), swapped[2], even)
    odd = jnp.where(early & (slab >= 1) & (slab < 3), swapped[1], swapped[0])
    before, after = before_and_after(even, odd, "slab")
    block = jnp.concatenate([before[z - 3 :], e_ref[...], after[:3]], axis=0)
    shape = ((sizes.rows + 4) * SUB, sizes.rows + 4)
    select = jnp.where(iota(shape, 1) == iota(shape, 0) // SUB, 1.0, 0.0).astype(BF16)
    for start in range(0, sizes.cols, SUB):
        e = block[:, start : start + SUB, :].reshape((z + 6) * SUB, wide)
        flat = e.astype(F32).T
        count = sizes.rows + 4
        flat = jnp.concatenate([flat[shift : shift + count] for shift in range(3)], axis=1)
        picked = jnp.broadcast_to(flat[:, None, :], (count, SUB, flat.shape[1])).reshape(count * SUB, flat.shape[1])
        same = iota(picked.shape, 1) % SUB == iota(picked.shape, 0) % SUB
        picked = jnp.where(same, picked, 0.0)
        two = hidden_layers(picked, w1, w2, c1, c2, low, high)
        lanes = two.shape[1]
        tall = jnp.concatenate([two, jnp.zeros((sizes.slot * SUB - two.shape[0], lanes), F32)], axis=0)
        tall = tall.reshape(sizes.slot, SUB, lanes).transpose(1, 0, 2).reshape(SUB * sizes.slot, lanes)
        total = last_layer(w3, tall.astype(BF16))
        rest = jnp.zeros((total.shape[0], LANES - sizes.rows), F32)
        for x in range(SUB):
            piece = total[:, x * sizes.slot : x * sizes.slot + sizes.rows]
            turned[pl.ds(x, total.shape[0], stride=SUB), :] = jnp.concatenate([piece, rest], axis=1)
        here = slice(start, start + SUB)
        for s in range(z):
            yz = [turned[(g * z + s) * SUB : (g * z + s + 1) * SUB, : sizes.rows] for g in range(3)]
            out_ref[0, s, here, :] = base_ref[0, s, here, :] + yz[0]
            out_ref[1, s, here, :] = base_ref[1, s, here, :] + 0.5 * yz[1]
            out_ref[2, s, here, :] = base_ref[2, s, here, :]
            out_ref[3, s, here, :] = base_ref[3, s, here, :] + 0.5 * yz[2]


def call(kernel, name, outs, args, scratch=(), flops=0, space=pltpu.VMEM):
    single = not isinstance(outs, list)
    shapes = [jax.ShapeDtypeStruct(shape, kind) for shape, kind in ([outs] if single else outs)]
    return pl.pallas_call(
        kernel,
        name=name,
        out_shape=shapes[0] if single else shapes,
        in_specs=[pl.BlockSpec(memory_space=space)] * len(args),
        scratch_shapes=scratch,
        compiler_params=pltpu.CompilerParams(vmem_limit_bytes=LIMIT),
        cost_estimate=pl.CostEstimate(flops=flops, bytes_accessed=1 << 20, transcendentals=0),
    )(*args)


def local(image, first_kernel, first_bias, middle_kernel, middle_bias, last_kernel, last_bias):
    slices, rows, cols = image.shape
    channels, outputs = first_kernel.shape[2], last_kernel.shape[2]
    sizes = Sizes(slices, rows, cols, channels, outputs, lax.axis_size("slab"), lax.axis_size("row"))
    t = image.transpose(0, 2, 1)
    even, odd = swap_rows(t, 0), swap_rows(t, 1)
    parameters = (
        first_kernel.reshape(3, 3, channels),
        first_bias.reshape(1, channels),
        middle_kernel,
        middle_bias.reshape(1, channels),
        last_kernel,
        last_bias.reshape(1, outputs),
    )
    own, *weights = call(
        functools.partial(prepare_kernel, sizes),
        "prepare",
        [(t.shape, BF16), *sizes.weight_shapes()],
        [pltpu.with_memory_space_constraint(p, pltpu.HBM) for p in (t, *parameters)],
        [pltpu.VMEM(p.shape, p.dtype) for p in parameters] + [pltpu.SemaphoreType.DMA((7,))],
        flops=1 << 20,
        space=pltpu.HBM,
    )
    wide = rows + 6
    e = call(extend_kernel, "extend", ((slices, cols, wide), BF16), (own, even, odd))
    swapped = [swap_slabs(e, turn_of) for turn_of in (2, 1, 0)]
    lanes = max(kind[2][1] for kind in sizes.kinds) * channels
    xy_hidden = pltpu.VMEM(((sizes.span + SUB) * SUB, LANES), F32)
    base = call(
        functools.partial(xy_kernel, sizes),
        "xy",
        ((outputs + 1, slices, cols, rows), F32),
        (e, *weights[5:]),
        [xy_hidden] * pl.cdiv(lanes, LANES),
        flops=1 << 28,
    )
    flows = call(
        functools.partial(yz_kernel, sizes),
        "yz",
        ((outputs + 1, slices, cols, rows), F32),
        (e, *swapped, base, *weights[:5]),
        [pltpu.VMEM((sizes.padded * SUB, LANES), F32)],
        flops=1 << 28,
    )
    return flows.transpose(0, 1, 3, 2)


def solution(mesh):
    placed = (P("slab", "row", None), P(), P(), P(), P(), P(), P())
    return jax.shard_map(
        local, mesh=mesh, in_specs=placed, out_specs=P(None, "slab", "row", None), check_vma=False
    )
```

```python
import functools

import jax
import jax.numpy as jnp
from jax import lax
from jax.experimental import pallas as pl
from jax.experimental.pallas import tpu as pltpu
from jax.sharding import PartitionSpec as P

SUB = 8
LANES = 128
NEVER = -3.0e38
LIMIT = 12 << 20
F32 = jnp.float32
BF16 = jnp.bfloat16


def matching(count, parity):
    partner = {}
    for left in range(parity, count - 1, 2):
        partner[left] = left + 1
        partner[left + 1] = left
    return partner


def swap_rows(values, parity):
    count = lax.axis_size("row")
    partner = matching(count, parity)
    ends = [i for i in range(count) if i not in partner]
    for here, there in zip(ends, reversed(ends)):
        partner[here] = there
    return lax.ppermute(values, "row", sorted(partner.items()))


EARLY = 2


def slab_rounds(slabs, row):
    borders = list(range(slabs - 1))
    if row < EARLY:
        return [borders[:1] + borders[3::2], borders[1:2] + borders[4::2], borders[2:3]]
    return [borders[1::2], borders[::2], []]


def swap_slabs(values, turn_of):
    slabs, rows = lax.axis_size("slab"), lax.axis_size("row")
    across = matching(rows, 0)
    pairs = []
    for r in range(rows):
        partner = {}
        for border in slab_rounds(slabs, r)[turn_of]:
            partner[border], partner[border + 1] = border + 1, border
        for s in range(slabs):
            there = (partner[s], r) if s in partner else (s, across.get(r, r))
            pairs.append((s * rows + r, there[0] * rows + there[1]))
    return lax.ppermute(values, ("slab", "row"), sorted(pairs))


def before_and_after(even, odd, axis):
    here, count = lax.axis_index(axis), lax.axis_size(axis)
    low = here % 2 == 0
    before = jnp.where(low, odd, even)
    after = jnp.where(low, even, odd)
    before = jnp.where(here > 0, before, jnp.zeros_like(before))
    after = jnp.where(here < count - 1, after, jnp.zeros_like(after))
    return before, after


def tile_lanes(row, count):
    return jnp.concatenate([row] * count, axis=1)


def iota(shape, dim):
    return lax.broadcasted_iota(jnp.int32, shape, dim)


def nn(left, right):
    return lax.dot_general(left, right, (((1,), (0,)), ((), ())), preferred_element_type=F32)


def nt(left, right):
    return lax.dot_general(left, right, (((1,), (1,)), ((), ())), preferred_element_type=F32)


def last_layer(w3, hidden):
    every = nt(w3[...], hidden)
    count, lanes = every.shape[0] // 3, every.shape[1] - SUB
    return sum(every[i * count : (i + 1) * count, i : i + lanes] for i in range(3))


class Sizes:
    def __init__(self, slices, rows, cols, channels, outputs, slabs, parts):
        self.slices, self.rows, self.cols = slices, rows, cols
        self.channels, self.outputs = channels, outputs
        self.slabs, self.parts = slabs, parts
        assert slices >= 3 and SUB % slices == 0
        self.halves = SUB // slices
        assert rows % self.halves == 0 and cols % SUB == 0
        self.span = rows // self.halves
        self.padded = -(-outputs * slices // SUB) * SUB
        self.slot = rows + SUB
        self.chunks = []
        self.kinds = []
        for start in range(0, cols, SUB):
            ranges = []
            for reach in (3, 2, 1, 0):
                low = max(0, start - reach)
                ranges.append((low - start, min(cols, start + SUB + reach) - low))
            kind = tuple(ranges)
            if kind not in self.kinds:
                self.kinds.append(kind)
            self.chunks.append((start, self.kinds.index(kind)))

    def weight_shapes(self):
        c, z = self.channels, self.slices
        shapes = [
            ((3 * (z + 6) * SUB, (z + 4) * c), BF16),
            ((3, (z + 4) * c, (z + 2) * c), BF16),
            ((3 * self.padded, (z + 2) * c), BF16),
            ((1, (z + 4) * c), F32),
            ((1, (z + 2) * c), F32),
        ]
        for image, one, two, _ in self.kinds:
            shapes += [
                ((3 * z * image[1], one[1] * c), BF16),
                ((3, one[1] * c, two[1] * c), BF16),
                ((3 * self.outputs * SUB, two[1] * c), BF16),
                ((1, one[1] * c), F32),
                ((1, two[1] * c), F32),
            ]
        return shapes + [((self.outputs, SUB, self.rows), F32)]


def banded(blocks, out_count, in_count, offset):
    zero = jnp.zeros_like(blocks[0])
    lines = []
    for inner in range(in_count):
        line = []
        for out in range(out_count):
            tap = inner - out + offset
            line.append(blocks[tap] if 0 <= tap < 3 else zero)
        lines.append(jnp.concatenate(line, axis=1))
    return jnp.concatenate(lines, axis=0)


def spread(tap_of, group_of, shape, lines):
    total = jnp.zeros(shape, F32)
    for (group, tap), line in lines.items():
        total = jnp.where((tap_of == tap) & (group_of == group), line, total)
    return total.astype(BF16)


def prepare_kernel(sizes, *refs):
    count = 7
    arguments, outs, held, sems = refs[:count], refs[count:-count], refs[-count:-1], refs[-1]
    t_out, *outs = outs
    copies = [
        pltpu.make_async_copy(here, there, sems.at[i])
        for i, (here, there) in enumerate(zip(arguments, (t_out, *held)))
    ]
    for copy in copies:
        copy.start()
    for copy in copies:
        copy.wait()
    c, z, n_out = sizes.channels, sizes.slices, sizes.outputs
    k1_ref, b1_ref, k2_ref, b2_ref, k3_ref, b3_ref = held
    k1 = k1_ref[...].astype(F32)
    k3 = k3_ref[...].astype(F32)
    b1, b2 = b1_ref[...], b2_ref[...]

    k2 = [[k2_ref[a, b].astype(F32).T.astype(BF16) for b in range(3)] for a in range(3)]

    def first(ref, tap_of, tap_index):
        rows, lanes = ref.shape[0] // 3, ref.shape[1]
        for shift in range(3):
            lines = {(0, t): tile_lanes(k1[tap_index(shift, t)][None, :], lanes // c) for t in range(3)}
            ref[shift * rows : (shift + 1) * rows, :] = spread(tap_of, 0, (rows, lanes), lines)

    def last(shape, group_of, tap_of, tap_index, shift):
        lines = {
            (g, t): tile_lanes(k3[tap_index(shift, t)][g][None, :], shape[1] // c)
            for g in range(n_out)
            for t in range(3)
        }
        return spread(tap_of, group_of, shape, lines)

    def along_z(shift, t):
        return t, shift

    def along_x(shift, t):
        return shift, t

    w1, w2, w3, c1, c2 = outs[:5]
    shape = (w1.shape[0] // 3, w1.shape[1])
    first(w1, iota(shape, 0) // SUB - iota(shape, 1) // c, along_z)
    shape = (w3.shape[0] // 3, w3.shape[1])
    row = iota(shape, 0)
    for b in range(3):
        w2[b] = banded([k2[a][b] for a in range(3)], z + 2, z + 4, 0)
        w3[b * shape[0] : (b + 1) * shape[0], :] = last(
            shape, row // z, iota(shape, 1) // c - row % z, along_z, b
        )
    base = lax.axis_index("slab") * z
    for ref, bias, reach in ((c1, b1, 2), (c2, b2, 1)):
        where = base + iota(ref.shape, 1) // c - reach
        inside = (where >= 0) & (where < sizes.slabs * z)
        ref[...] = jnp.where(inside, tile_lanes(bias, ref.shape[1] // c), NEVER)

    for index, (image, one, two, out) in enumerate(sizes.kinds):
        w1, w2, w3, c1, c2 = outs[5 + 5 * index : 10 + 5 * index]
        shape = (w1.shape[0] // 3, w1.shape[1])
        first(w1, iota(shape, 0) % image[1] + image[0] - iota(shape, 1) // c - one[0] + 1, along_x)
        shape = (w3.shape[0] // 3, w3.shape[1])
        row = iota(shape, 0)
        tap = iota(shape, 1) // c + two[0] - row % SUB - out[0] + 1
        for a in range(3):
            w2[a] = banded([k2[a][b] for b in range(3)], two[1], one[1], one[0] - two[0] + 1)
            w3[a * shape[0] : (a + 1) * shape[0], :] = last(shape, row // SUB, tap, along_x, a)
        c1[...] = tile_lanes(b1, one[1])
        c2[...] = tile_lanes(b2, two[1])
    for g in range(n_out):
        outs[-1][g] = jnp.broadcast_to(b3_ref[0:1, g : g + 1], (SUB, sizes.rows))


def extend_kernel(own_ref, even_ref, odd_ref, out_ref):
    rows = own_ref.shape[2]
    here, count = lax.axis_index("row"), lax.axis_size("row")
    low = here % 2 == 0
    edge = jnp.concatenate([jnp.where(low, odd_ref[...], even_ref[...])[:, :, rows - 3 :], own_ref[...]], axis=2)
    every = jnp.concatenate([edge, jnp.where(low, even_ref[...], odd_ref[...])[:, :, :3]], axis=2)
    lane = iota(every.shape, 2)
    first = jnp.where(here > 0, 0, 3)
    final = jnp.where(here < count - 1, rows + 6, rows + 3)
    out_ref[...] = jnp.where((lane >= first) & (lane < final), every.astype(F32), 0.0).astype(BF16)


def zero_groups(values, count, low, high):
    edge = count * SUB
    top, middle, bottom = values[:edge], values[edge:-edge], values[-edge:]
    if low.ndim:
        low, high = low[:edge], high[:edge]
    return jnp.concatenate([jnp.where(low, 0.0, top), middle, jnp.where(high, 0.0, bottom)], axis=0)


def taps(values, count):
    low, high = values.astype(BF16), values[SUB:].astype(BF16)
    return [low[:count], high[:count], low[2 * SUB : 2 * SUB + count]]


def pick(select, e):
    count = select.shape[1]
    return nt(select, jnp.concatenate([e[:, shift : shift + count] for shift in range(3)], axis=0))


def hidden_layers(picked, w1, w2, c1, c2, low, high):
    n2 = picked.shape[0] - 2 * SUB
    one = nn(picked.astype(BF16), w1[...])
    one = zero_groups(jnp.maximum(one + c1[...], 0.0), 2, low, high)
    two = sum(nn(tap, w2[i]) for i, tap in enumerate(taps(one, n2)))
    return zero_groups(jnp.maximum(two + c2[...], 0.0), 1, low, high)


def xy_kernel(sizes, e_ref, *refs):
    count = sum(1 for _ in sizes.kinds) * 5
    weights, (b3, out_ref) = refs[:count], refs[count:]
    z, span = sizes.slices, sizes.span
    wide = sizes.rows + 6
    row = lax.axis_index("row")
    half = iota((2 * SUB, 1), 0) % SUB // z
    low = (row == 0) & (half == 0)
    high = (row == sizes.parts - 1) & (half == sizes.halves - 1)
    shape = ((span + 4) * SUB, sizes.rows + 4)
    wanted = iota(shape, 0) // SUB + iota(shape, 0) % SUB // z * span
    select = jnp.where(iota(shape, 1) == wanted, 1.0, 0.0).astype(BF16)
    for start, index in sizes.chunks:
        image = sizes.kinds[index][0]
        w1, w2, w3, c1, c2 = weights[5 * index : 5 * index + 5]
        low_col = start + image[0]
        e = e_ref[:, low_col : low_col + image[1], :].reshape(z * image[1], wide)
        picked = pick(select, e)
        same = iota(picked.shape, 1) // image[1] % z == iota(picked.shape, 0) % z
        picked = jnp.where(same, picked, 0.0)
        second = hidden_layers(picked, w1, w2, c1, c2, low, high)
        lanes, last = second.shape[1], sizes.halves - 1
        tall = jnp.concatenate([second, jnp.zeros((6 * SUB, lanes), F32)], axis=0)
        tall = tall.reshape(-1, SUB, lanes).transpose(1, 0, 2)
        parts = [
            tall[h * z + s, : span if h < last else span + SUB] for s in range(z) for h in range(sizes.halves)
        ]
        total = last_layer(w3, jnp.concatenate(parts, axis=0).astype(BF16))
        here = slice(start, start + SUB)
        for s in range(z):
            xy = [
                total[g * SUB : (g + 1) * SUB, s * sizes.slot : s * sizes.slot + sizes.rows] + b3[g] for g in range(3)
            ]
            out_ref[0, s, here, :] = b3[0]
            out_ref[1, s, here, :] = 0.5 * (xy[0] + b3[1])
            out_ref[2, s, here, :] = xy[1]
            out_ref[3, s, here, :] = 0.5 * (xy[2] + b3[2])


def yz_kernel(sizes, e_ref, round_2, round_1, round_0, base_ref, w1, w2, w3, c1, c2, out_ref, turned):
    z = sizes.slices
    wide = sizes.rows + 6
    row = lax.axis_index("row")
    low, high = row == 0, row == sizes.parts - 1
    slab = lax.axis_index("slab")
    early = lax.axis_index("row") < EARLY
    swapped = [ref[...] for ref in (round_0, round_1, round_2)]
    even = jnp.where(early & (slab < 2), swapped[0], swapped[1])
    even = jnp.where(early & (slab >= 2) & (slab < 4), swapped[2], even)
    odd = jnp.where(early & (slab >= 1) & (slab < 3), swapped[1], swapped[0])
    before, after = before_and_after(even, odd, "slab")
    block = jnp.concatenate([before[z - 3 :], e_ref[...], after[:3]], axis=0)
    shape = ((sizes.rows + 4) * SUB, sizes.rows + 4)
    select = jnp.where(iota(shape, 1) == iota(shape, 0) // SUB, 1.0, 0.0).astype(BF16)
    for start in range(0, sizes.cols, SUB):
        e = block[:, start : start + SUB, :].reshape((z + 6) * SUB, wide)
        flat = e.astype(F32).T
        count = sizes.rows + 4
        flat = jnp.concatenate([flat[shift : shift + count] for shift in range(3)], axis=1)
        picked = jnp.broadcast_to(flat[:, None, :], (count, SUB, flat.shape[1])).reshape(count * SUB, flat.shape[1])
        same = iota(picked.shape, 1) % SUB == iota(picked.shape, 0) % SUB
        picked = jnp.where(same, picked, 0.0)
        two = hidden_layers(picked, w1, w2, c1, c2, low, high)
        lanes = two.shape[1]
        tall = jnp.concatenate([two, jnp.zeros((sizes.slot * SUB - two.shape[0], lanes), F32)], axis=0)
        tall = tall.reshape(sizes.slot, SUB, lanes).transpose(1, 0, 2).reshape(SUB * sizes.slot, lanes)
        total = last_layer(w3, tall.astype(BF16))
        rest = jnp.zeros((total.shape[0], LANES - sizes.rows), F32)
        for x in range(SUB):
            piece = total[:, x * sizes.slot : x * sizes.slot + sizes.rows]
            turned[pl.ds(x, total.shape[0], stride=SUB), :] = jnp.concatenate([piece, rest], axis=1)
        here = slice(start, start + SUB)
        for s in range(z):
            yz = [turned[(g * z + s) * SUB : (g * z + s + 1) * SUB, : sizes.rows] for g in range(3)]
            out_ref[0, s, here, :] = base_ref[0, s, here, :] + yz[0]
            out_ref[1, s, here, :] = base_ref[1, s, here, :] + 0.5 * yz[1]
            out_ref[2, s, here, :] = base_ref[2, s, here, :]
            out_ref[3, s, here, :] = base_ref[3, s, here, :] + 0.5 * yz[2]


def call(kernel, name, outs, args, scratch=(), flops=0, space=pltpu.VMEM):
    single = not isinstance(outs, list)
    shapes = [jax.ShapeDtypeStruct(shape, kind) for shape, kind in ([outs] if single else outs)]
    return pl.pallas_call(
        kernel,
        name=name,
        out_shape=shapes[0] if single else shapes,
        in_specs=[pl.BlockSpec(memory_space=space)] * len(args),
        scratch_shapes=scratch,
        compiler_params=pltpu.CompilerParams(vmem_limit_bytes=LIMIT),
        cost_estimate=pl.CostEstimate(flops=flops, bytes_accessed=1 << 20, transcendentals=0),
    )(*args)


def local(image, first_kernel, first_bias, middle_kernel, middle_bias, last_kernel, last_bias):
    slices, rows, cols = image.shape
    channels, outputs = first_kernel.shape[2], last_kernel.shape[2]
    sizes = Sizes(slices, rows, cols, channels, outputs, lax.axis_size("slab"), lax.axis_size("row"))
    t = image.transpose(0, 2, 1)
    even, odd = swap_rows(t, 0), swap_rows(t, 1)
    parameters = (
        first_kernel.reshape(3, 3, channels),
        first_bias.reshape(1, channels),
        middle_kernel,
        middle_bias.reshape(1, channels),
        last_kernel,
        last_bias.reshape(1, outputs),
    )
    own, *weights = call(
        functools.partial(prepare_kernel, sizes),
        "prepare",
        [(t.shape, BF16), *sizes.weight_shapes()],
        [pltpu.with_memory_space_constraint(p, pltpu.HBM) for p in (t, *parameters)],
        [pltpu.VMEM(p.shape, p.dtype) for p in parameters] + [pltpu.SemaphoreType.DMA((7,))],
        flops=1 << 20,
        space=pltpu.HBM,
    )
    wide = rows + 6
    e = call(extend_kernel, "extend", ((slices, cols, wide), BF16), (own, even, odd))
    swapped = [swap_slabs(e, turn_of) for turn_of in (2, 1, 0)]
    base = call(
        functools.partial(xy_kernel, sizes),
        "xy",
        ((outputs + 1, slices, cols, rows), F32),
        (e, *weights[5:]),
        flops=1 << 28,
    )
    flows = call(
        functools.partial(yz_kernel, sizes),
        "yz",
        ((outputs + 1, slices, cols, rows), F32),
        (e, *swapped, base, *weights[:5]),
        [pltpu.VMEM((sizes.padded * SUB, LANES), F32)],
        flops=1 << 28,
    )
    return flows.transpose(0, 1, 3, 2)


def solution(mesh):
    placed = (P("slab", "row", None), P(), P(), P(), P(), P(), P())
    return jax.shard_map(
        local, mesh=mesh, in_specs=placed, out_specs=P(None, "slab", "row", None), check_vma=False
    )
```
